32 devices in a mesh: beam: 8 (over y, x, core), mp: 4 (over z).
Axes of the slice: x: 2, y: 2, z: 4, core: 2. Of those that a mesh axis runs over, the one named last changes fastest.
Arguments:
- queries: bfloat16 [128, 128, 8192], P('beam', None, 'mp'), may hold values from -10 to 10
- new_kv: bfloat16 [128, 2, 128, 1024], P('beam', None, None, 'mp'), may hold values from -6 to 6
- newest_key_value: bfloat16 [128, 2, 128, 1024], P('beam', None, None, 'mp'), may hold values from -6 to 6
- ancestor_block_store: bfloat16 [96, 2, 128, 1024], P('beam', None, None, 'mp'), may hold values from -6 to 6
- parent: int32 [128], replicated, may hold values from 0 to 127, as said below
- ancestors: int32 [128, 5], P('beam'), may hold values from 0 to 95, as said below
- ancestor_count: int32 [128], P('beam'), may hold values from 1 to 5, as said below
- keep_list: int32 [64], replicated, may hold values from 0 to 127, as said below
- w_reward: bfloat16 [8192], P('mp'), may hold values from -0.0625 to 0.0625
Outputs:
- reward: float32 [128, 128], P('beam')
- kept_blocks: bfloat16 [64, 2, 128, 1024], P('beam', None, None, 'mp')
The draws below stay inside these ranges and needn't reach their ends.
Inputs may be any that keep to these rules, and one draw needn't show every extreme that they name: Each parent has exactly 2 children, consecutive beams of one device starting at a multiple of 2. The groups of children on one device have parents on distinct devices if there are at most as many groups on a device as devices; otherwise at most 2 groups share a parent device, and on every device some 2 do. `keep_list`: distinct beams; survivor j goes to device j // 8. The survivors bound for one device come from distinct devices if there are at most as many of them as devices; otherwise at most 2 come from one device, and on every device some 2 do. `ancestors`: 5 distinct blocks per beam, all among the 12 pool blocks held by the beam's own device. `ancestor_count`: every device has a beam with all 5 slots live.
All inputs are finite; a program needn't handle non-finite values.
Results may differ from the reference program's by a relative error of at most 0.0049.
Values may be sent and summed in bfloat16 or wider, within the bound.
No kernel may reach another device: no remote copies, remote signals or barrier semaphores. Data moves between devices by JAX's collectives and lax.ppermute only.
A program may use at most 128 MiB of HBM per device.

```python
import jax
import jax.numpy as jnp
import numpy as np
from jax import lax

QUERY_HEADS = 64
KEY_VALUE_HEADS = 8
HEAD_SIZE = 128
BLOCK_TOKENS = 128
CHILD = 2
ANC = 5
ANCESTOR_BLOCKS = 12
BEAM_DEV = 16
BEAM_TOTAL = 128
N_BEAM = 8


def source_table(key, salt):
    groups_dev = BEAM_DEV // CHILD
    paired = max(0, groups_dev - N_BEAM)
    random_base_key = jax.random.fold_in(key, salt)
    offset_perm = jax.random.permutation(jax.random.fold_in(random_base_key, 1), N_BEAM)
    outer_perm = jax.random.permutation(jax.random.fold_in(random_base_key, 2), N_BEAM)
    inner_perm = jax.random.permutation(jax.random.fold_in(random_base_key, 3), N_BEAM)
    index_table = jnp.array(np.array([g // 2 if g < 2 * paired else g - paired for g in range(groups_dev)], dtype=np.int32))
    offsets = offset_perm[index_table]
    sources = outer_perm[(inner_perm[:, None] + offsets[None, :]) % N_BEAM]
    within = jax.random.randint(jax.random.fold_in(random_base_key, 4), (N_BEAM, groups_dev), 0, CHILD)
    chosen = sources * BEAM_DEV + jnp.arange(groups_dev)[None, :] * CHILD + within
    ranking = jax.random.randint(jax.random.fold_in(random_base_key, 5), (N_BEAM, groups_dev), 0, 1 << 20) * groups_dev + jnp.arange(groups_dev)[None, :]
    ordering = jnp.argsort(ranking, axis=1)
    return jnp.take_along_axis(chosen, ordering, axis=1).astype(jnp.int32)


def draw_parent(key, part):
    return jnp.repeat(source_table(key, 17).reshape(-1), CHILD).astype(jnp.int32)


def draw_keep_list(key, part):
    return source_table(key, 29).reshape(-1).astype(jnp.int32)


def draw_ancestors(key, part):
    ranking = jax.random.randint(jax.random.fold_in(key, 31), (BEAM_TOTAL, ANCESTOR_BLOCKS), 0, 1 << 20) * ANCESTOR_BLOCKS + jnp.arange(ANCESTOR_BLOCKS)[None, :]
    local_ids = jnp.argsort(ranking, axis=1)[:, :ANC]
    return (local_ids + (jnp.arange(BEAM_TOTAL) // BEAM_DEV)[:, None] * ANCESTOR_BLOCKS).astype(jnp.int32)


def draw_ancestor_count(key, part):
    lengths = jax.random.randint(jax.random.fold_in(key, 37), (BEAM_TOTAL,), 1, ANC + 1)
    full_at = jax.random.randint(jax.random.fold_in(key, 38), (N_BEAM,), 0, BEAM_DEV)
    position = jnp.arange(BEAM_TOTAL) % BEAM_DEV
    device_of = jnp.arange(BEAM_TOTAL) // BEAM_DEV
    return jnp.where(position == full_at[device_of], ANC, lengths).astype(jnp.int32)


def draw_queries(key, part):
    random_base_key = jax.random.fold_in(key, 41)
    value_entries = 2.5 * jax.random.truncated_normal(jax.random.fold_in(random_base_key, 1), -4.0, 4.0, (BEAM_TOTAL, BLOCK_TOKENS, QUERY_HEADS * HEAD_SIZE), jnp.float32)
    return value_entries.astype(jnp.bfloat16)


def draw_new_kv(key, part):
    random_base_key = jax.random.fold_in(key, 53)
    value_entries = jax.random.truncated_normal(jax.random.fold_in(random_base_key, 1), -6.0, 6.0, (BEAM_TOTAL, 2, BLOCK_TOKENS, KEY_VALUE_HEADS * HEAD_SIZE), jnp.float32)
    return value_entries.astype(jnp.bfloat16)


def steps_of(own_key, shape, cuts, low, high):
    loudness = 1.0
    for dim, parts in cuts:
        heights = jax.random.uniform(jax.random.fold_in(jax.random.fold_in(own_key, 6), dim), (parts,), jnp.float32, low / len(cuts), high / len(cuts))
        loudness = loudness * jnp.repeat(jnp.exp(heights), shape[dim] // parts).reshape((-1,) + (1,) * (len(shape) - 1 - dim))
    return loudness


def gaussian(own_key, dims, scale, reach, split=(), kind=jnp.bfloat16):
    drawn = jax.random.normal(own_key, dims, jnp.float32) * scale
    if len(split) > 0:
        drawn = steps_of(own_key, dims, split, -0.22, 0.18) * drawn
    return jnp.clip(drawn, min=-reach, max=reach).astype(kind)


def setup_inputs(seed: int = 0) -> dict:
    key_list = jax.random.split(jax.random.key(seed), 10)
    queries = draw_queries(jax.random.fold_in(key_list[9], 71), 0)
    new_kv = draw_new_kv(jax.random.fold_in(key_list[9], 71), 0)
    newest_key_value = gaussian(key_list[2], (BEAM_TOTAL, 2, BLOCK_TOKENS, KEY_VALUE_HEADS * HEAD_SIZE), 1.0, 6.0, ((0, 8), (3, 4)))
    ancestor_block_store = gaussian(key_list[3], (N_BEAM * ANCESTOR_BLOCKS, 2, BLOCK_TOKENS, KEY_VALUE_HEADS * HEAD_SIZE), 1.0, 6.0, ((0, 8), (3, 4)))
    parent = draw_parent(jax.random.fold_in(key_list[9], 71), 0)
    ancestors = draw_ancestors(jax.random.fold_in(key_list[9], 71), 0)
    ancestor_count = draw_ancestor_count(jax.random.fold_in(key_list[9], 71), 0)
    keep_list = draw_keep_list(jax.random.fold_in(key_list[9], 71), 0)
    w_reward = gaussian(key_list[8], (QUERY_HEADS * HEAD_SIZE,), (QUERY_HEADS * HEAD_SIZE) ** -0.5, 0.0625, ((0, 4),))
    return dict(queries=queries, new_kv=new_kv, newest_key_value=newest_key_value, ancestor_block_store=ancestor_block_store, parent=parent, ancestors=ancestors, ancestor_count=ancestor_count, keep_list=keep_list, w_reward=w_reward)


def reference(queries, new_kv, newest_key_value, ancestor_block_store, parent, ancestors, ancestor_count, keep_list, w_reward):
    scale_factor = HEAD_SIZE ** -0.5
    query_groups_per_head = QUERY_HEADS // KEY_VALUE_HEADS
    total_key_count = (ANC + 2) * BLOCK_TOKENS
    key_slot = jnp.arange(total_key_count) // BLOCK_TOKENS
    key_pos = jnp.arange(total_key_count) % BLOCK_TOKENS
    tok_pos = jnp.arange(BLOCK_TOKENS)
    parent_kv = jnp.take(newest_key_value, parent, axis=0)

    def attend_beam(pieces):
        current_query_block, own_block, parent_block, block_ids, live_count = pieces
        block_list = jnp.concatenate([jnp.take(ancestor_block_store, block_ids, axis=0), parent_block[None], own_block[None]], axis=0)
        key_row_matrix = block_list[:, 0].reshape(total_key_count, KEY_VALUE_HEADS, HEAD_SIZE).astype(jnp.float32)
        value_row_matrix = block_list[:, 1].reshape(total_key_count, KEY_VALUE_HEADS, HEAD_SIZE).astype(jnp.float32)
        query_row_matrix = current_query_block.reshape(BLOCK_TOKENS, KEY_VALUE_HEADS, query_groups_per_head, HEAD_SIZE).astype(jnp.float32)
        scores = jnp.einsum("tkgd,jkd->kgtj", query_row_matrix, key_row_matrix) * scale_factor
        allowed = jnp.where((key_slot < ANC)[None, :], (key_slot < live_count)[None, :],
                            jnp.where((key_slot == ANC)[None, :], True, key_pos[None, :] <= tok_pos[:, None]))
        scores = jnp.where(allowed[None, None], scores, -jnp.inf)
        highest = jnp.max(scores, axis=-1, keepdims=True)
        weights = jnp.exp(scores - highest)
        probabilities = (weights / jnp.sum(weights, axis=-1, keepdims=True)).astype(jnp.bfloat16)
        probabilities = lax.optimization_barrier(probabilities).astype(jnp.float32)
        mixture = jnp.einsum("kgtj,jkd->tkgd", probabilities, value_row_matrix)
        attended = mixture.astype(jnp.bfloat16).reshape(BLOCK_TOKENS, QUERY_HEADS * HEAD_SIZE)
        return jnp.dot(attended, w_reward, preferred_element_type=jnp.float32)

    reward = lax.map(attend_beam, (queries, new_kv, parent_kv, ancestors, ancestor_count))
    kept_blocks = jnp.take(new_kv, keep_list, axis=0)
    return reward, kept_blocks
```

```python
import functools
import math

import jax
import jax.numpy as jnp
from jax import lax
from jax.experimental import pallas as pl
from jax.experimental.pallas import tpu as pltpu
from jax.sharding import PartitionSpec as P

HEAD_SIZE = 128
CHILD = 2
LOG2_SCALE = HEAD_SIZE ** (-0.5) * math.log2(math.e)
MASKED = -1e30
LANES_BOTH = 2 * HEAD_SIZE
ANY = pl.BlockSpec(memory_space=pl.ANY)


def find_row(table, start, step, count, own_index, beam_dev):
    def look(i, found):
        beam = table[start + i * step]
        return jnp.where(beam // beam_dev == own_index, beam % beam_dev, found)

    return lax.fori_loop(0, count, look, jnp.int32(0))


def pack_kernel(
    own_ref,
    parent_ref,
    keep_ref,
    weight_ref,
    newest_ref,
    new_ref,
    parent_out,
    keep_out,
    value_buf,
    sum_buf,
    keep_sem,
    key_sem,
    value_sem,
    sum_sem,
    *,
    devices,
    beam_dev,
    keep_dev,
):
    groups = beam_dev // CHILD
    own = own_ref[0]
    tokens = newest_ref.shape[2]
    kv_heads = newest_ref.shape[3] // HEAD_SIZE
    heads = weight_ref.shape[0]
    per_group = heads // kv_heads

    def value_copy(d, row):
        return pltpu.make_async_copy(
            newest_ref.at[row, 1], value_buf.at[d], value_sem.at[d]
        )

    def key_copy(d, row):
        return pltpu.make_async_copy(
            newest_ref.at[row, 0], parent_out.at[d, pl.ds(0, tokens)], key_sem.at[d]
        )

    def keep_copy(d, kept):
        return pltpu.make_async_copy(new_ref.at[kept], keep_out.at[d], keep_sem.at[d])

    @pl.loop(0, devices)
    def _(d):
        row = find_row(parent_ref, d * beam_dev, CHILD, groups, own, beam_dev)
        kept = find_row(keep_ref, d * keep_dev, 1, keep_dev, own, beam_dev)
        value_copy(d, row).start()
        key_copy(d, row).start()
        keep_copy(d, kept).start()

    def sums_copy(d):
        return pltpu.make_async_copy(
            sum_buf.at[d],
            parent_out.at[d, pl.ds(tokens, 2 * per_group)],
            sum_sem.at[d],
        )

    @pl.loop(0, devices)
    def _(d):
        value_copy(d, 0).wait()
        for kv in range(kv_heads):
            total = lax.dot_general(
                weight_ref[kv * per_group : (kv + 1) * per_group],
                value_buf[d, :, kv * HEAD_SIZE : (kv + 1) * HEAD_SIZE],
                (((1,), (1,)), ((), ())),
                preferred_element_type=jnp.float32,
            )
            high = total.astype(jnp.bfloat16)
            low = (total - high.astype(jnp.float32)).astype(jnp.bfloat16)
            lanes = slice(kv * tokens, (kv + 1) * tokens)
            sum_buf[d, :per_group, lanes] = high
            sum_buf[d, per_group:, lanes] = low
        sums_copy(d).start()

    @pl.loop(0, devices)
    def _(d):
        key_copy(d, 0).wait()
        keep_copy(d, 0).wait()
        sums_copy(d).wait()


def online_step(scores, sums, state, pair):
    highest, top, bottom = state
    scores = scores.reshape(-1, 8, scores.shape[-1])
    sums = sums.reshape(scores.shape)
    before = highest[pair]
    after = jnp.maximum(before, jnp.max(scores, axis=0))
    fade = jnp.exp2((before - after) * LOG2_SCALE)
    weights = jnp.exp2((scores - after[None]) * LOG2_SCALE)
    return (
        after,
        top[pair] * fade + jnp.sum(weights * sums, axis=0),
        bottom[pair] * fade + jnp.sum(weights, axis=0),
    )


def query_pair(query_ref, pair):
    start = pair * LANES_BOTH
    return jnp.concatenate(
        [
            query_ref[0, :, start : start + HEAD_SIZE],
            query_ref[0, :, start + HEAD_SIZE : start + LANES_BOTH],
        ],
        axis=0,
    )


def key_scores(keys, query):
    return lax.dot_general(
        keys, query, (((1,), (1,)), ((), ())), preferred_element_type=jnp.float32
    )


def local_kernel(
    block_ids,
    live_count,
    query_ref,
    own_ref,
    store_ref,
    spread_ref,
    state_ref,
    sums_ref,
    *,
    pairs,
    pairs_kv,
):
    beam = pl.program_id(0)
    blocks = store_ref.shape[0]
    tokens = store_ref.shape[2]

    def spread_sums(values, pair):
        return jnp.dot(
            values,
            spread_ref[:, pair * LANES_BOTH : (pair + 1) * LANES_BOTH],
            preferred_element_type=jnp.float32,
        )

    def lanes(pair):
        kv = pair // pairs_kv
        return slice(kv * HEAD_SIZE, (kv + 1) * HEAD_SIZE)

    @pl.when(beam == 0)
    def _():
        @pl.loop(0, blocks)
        def _(block):
            for pair in range(pairs):
                sums_ref[block, pair] = spread_sums(
                    store_ref[block, 1, :, lanes(pair)], pair
                )

    state = (state_ref.at[0, 0], state_ref.at[0, 1], state_ref.at[0, 2])
    state_ref[0, 0] = jnp.full(state_ref.shape[2:], MASKED, jnp.float32)
    state_ref[0, 1] = jnp.zeros(state_ref.shape[2:], jnp.float32)
    state_ref[0, 2] = jnp.zeros(state_ref.shape[2:], jnp.float32)

    def update(pair, scores, sums):
        highest, top, bottom = online_step(scores, sums, state, pair)
        state_ref[0, 0, pair] = highest
        state_ref[0, 1, pair] = top
        state_ref[0, 2, pair] = bottom

    @pl.loop(0, live_count[beam])
    def _(slot):
        block = block_ids[beam, slot]
        for pair in range(pairs):
            scores = key_scores(
                store_ref[block, 0, :, lanes(pair)], query_pair(query_ref, pair)
            )
            update(pair, scores, sums_ref[block, pair])

    shape = (tokens, LANES_BOTH)
    key_pos = lax.broadcasted_iota(jnp.int32, shape, 0)
    token_pos = lax.broadcasted_iota(jnp.int32, shape, 1) % tokens
    allowed = key_pos <= token_pos
    for pair in range(pairs):
        scores = key_scores(own_ref[0, 0, :, lanes(pair)], query_pair(query_ref, pair))
        scores = jnp.where(allowed, scores, MASKED)
        update(pair, scores, spread_sums(own_ref[0, 1, :, lanes(pair)], pair))


def parent_kernel(
    source,
    query_ref,
    state_ref,
    parent_ref,
    select_ref,
    reward_ref,
    sums_ref,
    *,
    pairs,
    pairs_kv,
):
    beam = pl.program_id(0)
    sum_rows = select_ref.shape[0]
    tokens = parent_ref.shape[1] - sum_rows

    @pl.when(beam % CHILD == 0)
    def _():
        for pair in range(pairs):
            kv = pair // pairs_kv
            start = (pair % pairs_kv) * LANES_BOTH
            sums_ref[pair] = lax.dot_general(
                parent_ref[0, pl.ds(tokens, sum_rows), kv * tokens : (kv + 1) * tokens],
                select_ref[:, start : start + LANES_BOTH],
                (((0,), (0,)), ((), ())),
                preferred_element_type=jnp.float32,
            )

    state = (state_ref.at[0, 0], state_ref.at[0, 1], state_ref.at[0, 2])
    total = jnp.zeros((1, tokens), jnp.float32)
    for pair in range(pairs):
        kv = pair // pairs_kv
        scores = key_scores(
            parent_ref[0, pl.ds(0, tokens), kv * HEAD_SIZE : (kv + 1) * HEAD_SIZE],
            query_pair(query_ref, pair),
        )
        highest, top, bottom = online_step(scores, sums_ref[pair], state, pair)
        row_max = jnp.max(highest, axis=0, keepdims=True)
        fade = jnp.exp2((highest - row_max) * LOG2_SCALE)
        ratio = jnp.sum(top * fade, axis=0, keepdims=True) / jnp.sum(
            bottom * fade, axis=0, keepdims=True
        )
        total = total + ratio[:, :tokens] + ratio[:, tokens:]
    reward_ref[pl.ds(beam, 1), :] = total


def place_kernel(source, landed_ref, kept_ref, sems, *, keep_dev):
    def copy(j):
        return pltpu.make_async_copy(
            landed_ref.at[source[j]], kept_ref.at[j], sems.at[j]
        )

    for j in range(keep_dev):
        copy(j).start()
    for j in range(keep_dev):
        copy(j).wait()


def on_device(
    queries,
    new_kv,
    newest_key_value,
    ancestor_block_store,
    parent,
    ancestors,
    ancestor_count,
    keep_list,
    w_reward,
):
    devices = lax.axis_size("beam")
    mp = lax.axis_size("mp")
    own = lax.axis_index("beam")
    beam_dev, _, tokens, kv_width = new_kv.shape
    q_width = queries.shape[2]
    heads = q_width // HEAD_SIZE
    kv_heads = kv_width // HEAD_SIZE
    pairs = heads // 2
    pairs_kv = pairs // kv_heads
    keep_dev = keep_list.shape[0] // devices
    blocks = ancestor_block_store.shape[0]
    slots = ancestors.shape[1]
    per_group = heads // kv_heads
    sum_rows = 2 * per_group

    weight = w_reward.reshape(heads, HEAD_SIZE)
    parent_out, keep_out = pl.pallas_call(
        functools.partial(
            pack_kernel, devices=devices, beam_dev=beam_dev, keep_dev=keep_dev
        ),
        out_shape=(
            jax.ShapeDtypeStruct((devices, tokens + sum_rows, kv_width), jnp.bfloat16),
            jax.ShapeDtypeStruct((devices, 2, tokens, kv_width), jnp.bfloat16),
        ),
        grid_spec=pltpu.PrefetchScalarGridSpec(
            num_scalar_prefetch=3,
            grid=(1,),
            in_specs=[
                pl.BlockSpec((heads, HEAD_SIZE), lambda i, *_: (0, 0)),
                ANY,
                ANY,
            ],
            out_specs=(ANY, ANY),
            scratch_shapes=[
                pltpu.VMEM((devices, tokens, kv_width), jnp.bfloat16),
                pltpu.VMEM((devices, sum_rows, kv_width), jnp.bfloat16),
                pltpu.SemaphoreType.DMA((devices,)),
                pltpu.SemaphoreType.DMA((devices,)),
                pltpu.SemaphoreType.DMA((devices,)),
                pltpu.SemaphoreType.DMA((devices,)),
            ],
        ),
        name="pack",
    )(own.reshape(1), parent, keep_list, weight, newest_key_value, new_kv)

    arrived = lax.all_to_all(parent_out, "beam", split_axis=0, concat_axis=0, tiled=True)
    landed = lax.all_to_all(keep_out, "beam", split_axis=0, concat_axis=0, tiled=True)

    spread = jnp.repeat(weight.T, HEAD_SIZE, axis=1)
    local_ids = ancestors - own * blocks
    state_shape = (beam_dev, 3, pairs, 8, LANES_BOTH)
    state_block = (1,) + state_shape[1:]
    state = pl.pallas_call(
        functools.partial(local_kernel, pairs=pairs, pairs_kv=pairs_kv),
        out_shape=jax.ShapeDtypeStruct(state_shape, jnp.float32),
        grid_spec=pltpu.PrefetchScalarGridSpec(
            num_scalar_prefetch=2,
            grid=(beam_dev,),
            in_specs=[
                pl.BlockSpec((1, tokens, q_width), lambda b, *_: (b, 0, 0)),
                pl.BlockSpec((1, 2, tokens, kv_width), lambda b, *_: (b, 0, 0, 0)),
                pl.BlockSpec(
                    ancestor_block_store.shape,
                    lambda b, *_: (0, 0, 0, 0),
                    pipeline_mode=pl.Buffered(1),
                ),
                pl.BlockSpec(
                    spread.shape, lambda b, *_: (0, 0), pipeline_mode=pl.Buffered(1)
                ),
            ],
            out_specs=pl.BlockSpec(state_block, lambda b, *_: (b, 0, 0, 0, 0)),
            scratch_shapes=[
                pltpu.VMEM((blocks, pairs, tokens, LANES_BOTH), jnp.float32)
            ],
        ),
        name="local",
    )(local_ids, ancestor_count, queries, new_kv, ancestor_block_store, spread)

    own_parents = lax.dynamic_slice(parent, (own * beam_dev,), (beam_dev,))
    source = own_parents // beam_dev
    head_ids = jnp.arange(sum_rows) % per_group
    lane_heads = jnp.arange(per_group * HEAD_SIZE) // HEAD_SIZE
    select = (head_ids[:, None] == lane_heads[None, :]).astype(jnp.bfloat16)
    partial_reward = pl.pallas_call(
        functools.partial(parent_kernel, pairs=pairs, pairs_kv=pairs_kv),
        out_shape=jax.ShapeDtypeStruct((beam_dev, tokens), jnp.float32),
        grid_spec=pltpu.PrefetchScalarGridSpec(
            num_scalar_prefetch=1,
            grid=(beam_dev,),
            in_specs=[
                pl.BlockSpec((1, tokens, q_width), lambda b, *_: (b, 0, 0)),
                pl.BlockSpec(state_block, lambda b, *_: (b, 0, 0, 0, 0)),
                pl.BlockSpec(
                    (1, tokens + sum_rows, kv_width),
                    lambda b, source: (source[b], 0, 0),
                ),
                pl.BlockSpec(
                    select.shape, lambda b, *_: (0, 0), pipeline_mode=pl.Buffered(1)
                ),
            ],
            out_specs=pl.BlockSpec((beam_dev, tokens), lambda b, *_: (0, 0)),
            scratch_shapes=[pltpu.VMEM((pairs, tokens, LANES_BOTH), jnp.float32)],
        ),
        name="parents",
    )(source, queries, state, arrived, select)

    keep_source = (
        lax.dynamic_slice(keep_list, (own * keep_dev,), (keep_dev,)) // beam_dev
    )
    kept_blocks = pl.pallas_call(
        functools.partial(place_kernel, keep_dev=keep_dev),
        out_shape=jax.ShapeDtypeStruct((keep_dev,) + new_kv.shape[1:], new_kv.dtype),
        grid_spec=pltpu.PrefetchScalarGridSpec(
            num_scalar_prefetch=1,
            grid=(1,),
            in_specs=[ANY],
            out_specs=ANY,
            scratch_shapes=[pltpu.SemaphoreType.DMA((keep_dev,))],
        ),
        name="place",
    )(keep_source, landed)

    reward = partial_reward
    for shift in range(1, mp):
        ring = [(i, (i + shift) % mp) for i in range(mp)]
        reward = reward + lax.ppermute(partial_reward, "mp", ring)
    return (reward, kept_blocks)


def solution(mesh):
    placed = (
        P("beam", None, "mp"),
        P("beam", None, None, "mp"),
        P("beam", None, None, "mp"),
        P("beam", None, None, "mp"),
        P(),
        P("beam", None),
        P("beam"),
        P(),
        P("mp"),
    )
    return jax.shard_map(
        on_device,
        mesh=mesh,
        in_specs=placed,
        out_specs=(P("beam", None), P("beam", None, None, "mp")),
        check_vma=False,
    )
```

```python
import functools
import math

import jax
import jax.numpy as jnp
from jax import lax
from jax.experimental import pallas as pl
from jax.experimental.pallas import tpu as pltpu
from jax.sharding import PartitionSpec as P

HEAD_SIZE = 128
CHILD = 2
LOG2_SCALE = HEAD_SIZE ** (-0.5) * math.log2(math.e)
MASKED = -1e30
SAFE_LOW = 2.0**-60
SAFE_HIGH = 2.0**100
LANES_BOTH = 2 * HEAD_SIZE
ANY = pl.BlockSpec(memory_space=pl.ANY)


def dot_last(a, b):
    return lax.dot_general(
        a, b, (((1,), (1,)), ((), ())), preferred_element_type=jnp.float32
    )


def dot_first(a, b):
    return lax.dot_general(
        a, b, (((0,), (0,)), ((), ())), preferred_element_type=jnp.float32
    )


def one_hot_rows(rows, period, first):
    shape = (rows, LANES_BOTH)
    row = lax.broadcasted_iota(jnp.int32, shape, 0) % period
    head = first + lax.broadcasted_iota(jnp.int32, shape, 1) // HEAD_SIZE
    return jnp.where(row == head, 1.0, 0.0).astype(jnp.bfloat16)


def split_keys(keys):
    scaled = keys.astype(jnp.float32) * LOG2_SCALE
    high = scaled.astype(jnp.bfloat16)
    low = (scaled - high.astype(jnp.float32)).astype(jnp.bfloat16)
    return jnp.concatenate([high, low], axis=1)


def kv_lanes(kv):
    return slice(kv * HEAD_SIZE, (kv + 1) * HEAD_SIZE)


def stack_queries(query_ref, stacked_ref, pairs):
    for pair in range(pairs):
        for side in range(2):
            head = 2 * pair + side
            stacked_ref[pair, side * HEAD_SIZE : (side + 1) * HEAD_SIZE] = query_ref[
                0, :, head * HEAD_SIZE : (head + 1) * HEAD_SIZE
            ]


def plain_block(keys, query, sums, allowed=None):
    scores = dot_last(keys, jnp.concatenate([query, query], axis=1))
    if allowed is not None:
        scores = jnp.where(allowed, scores, MASKED)
    weights = jnp.exp2(scores).reshape(-1, 8, LANES_BOTH)
    return (
        jnp.sum(weights * sums.reshape(weights.shape), axis=0),
        jnp.sum(weights, axis=0),
    )


def causal(tokens):
    shape = (tokens, LANES_BOTH)
    key_pos = lax.broadcasted_iota(jnp.int32, shape, 0)
    token_pos = lax.broadcasted_iota(jnp.int32, shape, 1) % tokens
    return key_pos <= token_pos


def find_row(table, start, step, count, own_index, beam_dev):
    found = jnp.int32(0)
    for i in range(count):
        beam = table[start + i * step]
        found = jnp.where(beam // beam_dev == own_index, beam % beam_dev, found)
    return found


def pack_kernel(own_ref, parent_ref, keep_ref, weight_ref, newest_ref, new_ref, *rest, beam_dev, keep_dev):
    devices = len(rest) - 5
    outs = rest[:devices]
    pack_buf, value_buf, value_sem, rest_sem, out_sem = rest[devices:]
    groups = beam_dev // CHILD
    own = own_ref[0]
    tokens = newest_ref.shape[2]
    kv_heads = newest_ref.shape[3] // HEAD_SIZE
    per_group = weight_ref.shape[0] // kv_heads

    def loads(k, row, kept):
        return (
            pltpu.make_async_copy(
                newest_ref.at[row, 0],
                pack_buf.at[k, pl.ds(2 * tokens, tokens)],
                rest_sem.at[k, 0],
            ),
            pltpu.make_async_copy(
                new_ref.at[kept, 0], pack_buf.at[k, pl.ds(0, tokens)], rest_sem.at[k, 1]
            ),
            pltpu.make_async_copy(
                new_ref.at[kept, 1],
                pack_buf.at[k, pl.ds(tokens, tokens)],
                rest_sem.at[k, 2],
            ),
            pltpu.make_async_copy(
                newest_ref.at[row, 1], value_buf.at[k], value_sem.at[k]
            ),
        )

    @pl.loop(0, devices)
    def _(k):
        peer = own ^ k
        row = find_row(parent_ref, peer * beam_dev, CHILD, groups, own, beam_dev)
        kept = find_row(keep_ref, peer * keep_dev, 1, keep_dev, own, beam_dev)
        for copy in loads(k, row, kept):
            copy.start()

    for k in range(devices - 1, -1, -1):
        for copy in loads(k, 0, 0):
            copy.wait()
        for kv in range(kv_heads):
            total = dot_last(
                weight_ref[kv * per_group : (kv + 1) * per_group],
                value_buf[k, :, kv_lanes(kv)],
            )
            high = total.astype(jnp.bfloat16)
            low = (total - high.astype(jnp.float32)).astype(jnp.bfloat16)
            pack_buf[k, 3 * tokens : 3 * tokens + per_group, kv_lanes(kv)] = high
            pack_buf[k, 3 * tokens + per_group :, kv_lanes(kv)] = low
        pltpu.make_async_copy(pack_buf.at[k], outs[k], out_sem.at[k]).start()
    for k in range(devices):
        pltpu.make_async_copy(pack_buf.at[k], outs[k], out_sem.at[k]).wait()


def local_kernel(
    own_ref,
    block_ids,
    live_count,
    query_ref,
    new_ref,
    store_ref,
    weight_ref,
    state_ref,
    spread_ref,
    keys_ref,
    sums_ref,
    stacked_ref,
    *,
    pairs,
    pairs_kv,
):
    beam = pl.program_id(0)
    blocks = store_ref.shape[0]
    tokens = store_ref.shape[2]
    heads = weight_ref.shape[0]
    kv_heads = pairs // pairs_kv

    @pl.when(beam == 0)
    def _():
        for pair in range(pairs):
            spread_ref[pair] = dot_first(
                weight_ref[...], one_hot_rows(heads, heads, 2 * pair)
            ).astype(jnp.bfloat16)

        @pl.loop(0, blocks)
        def _(block):
            for kv in range(kv_heads):
                keys_ref[block, kv] = split_keys(store_ref[block, 0, :, kv_lanes(kv)])
            for pair in range(pairs):
                sums_ref[block, pair] = jnp.dot(
                    store_ref[block, 1, :, kv_lanes(pair // pairs_kv)],
                    spread_ref[pair],
                    preferred_element_type=jnp.float32,
                )

    stack_queries(query_ref, stacked_ref, pairs)
    allowed = causal(tokens)
    own_keys = [split_keys(new_ref[0, 0, :, kv_lanes(kv)]) for kv in range(kv_heads)]
    for pair in range(pairs):
        kv = pair // pairs_kv
        sums = jnp.dot(
            new_ref[0, 1, :, kv_lanes(kv)],
            spread_ref[pair],
            preferred_element_type=jnp.float32,
        )
        top, bottom = plain_block(own_keys[kv], stacked_ref[pair], sums, allowed)
        state_ref[0, 0, pair] = top
        state_ref[0, 1, pair] = bottom

    @pl.loop(0, live_count[beam])
    def _(slot):
        block = block_ids[beam, slot] - own_ref[0] * blocks
        for pair in range(pairs):
            top, bottom = plain_block(
                keys_ref[block, pair // pairs_kv],
                stacked_ref[pair],
                sums_ref[block, pair],
            )
            state_ref[0, 0, pair] += top
            state_ref[0, 1, pair] += bottom


def parent_kernel(own_ref, parent_ref, keep_ref, block_ids, live_count, *rest, devices, pairs, pairs_kv):
    query_ref, state_ref, weight_ref, query_any, new_any, store_any = rest[:6]
    arrived = rest[6 : 6 + devices]
    reward_ref, kept_ref = rest[6 + devices : 8 + devices]
    (
        parent_buf,
        kept_buf,
        keys_ref,
        sums_ref,
        stacked_ref,
        range_ref,
        slow_query,
        slow_block,
        slow_state,
        parent_sem,
        load_sem,
        store_sem,
        slow_sem,
    ) = rest[8 + devices :]
    beam = pl.program_id(0)
    beams = pl.num_programs(0)
    own = own_ref[0]
    keep_dev = kept_ref.shape[0]
    tokens = query_ref.shape[1]
    kv_heads = pairs // pairs_kv
    blocks = store_any.shape[0]
    sum_rows = parent_buf.shape[1] - tokens
    heads = 2 * pairs

    def parent_load(k):
        return pltpu.make_async_copy(
            arrived[k].at[pl.ds(2 * tokens, tokens + sum_rows)],
            parent_buf.at[k],
            parent_sem.at[k],
        )

    def kept_load(k):
        return pltpu.make_async_copy(
            arrived[k].at[pl.ds(0, 2 * tokens)], kept_buf.at[k], load_sem.at[k]
        )

    def kept_stores(j, k):
        return [
            pltpu.make_async_copy(
                kept_buf.at[k, pl.ds(side * tokens, tokens)],
                kept_ref.at[j, side],
                store_sem.at[j, side],
            )
            for side in range(2)
        ]

    @pl.when(beam == 0)
    def _():
        for k in range(devices):
            parent_load(k).start()
        for k in range(devices):
            kept_load(k).start()
        for k in range(devices):
            parent_load(k).wait()

    @pl.when(beam == 1)
    def _():
        for k in range(devices):
            kept_load(k).wait()

        @pl.loop(0, keep_dev)
        def _(j):
            k = (keep_ref[own * keep_dev + j] // beams) ^ own
            for copy in kept_stores(j, k):
                copy.start()

    def slot_of(b):
        return (parent_ref[own * beams + b] // beams) ^ own

    slot = slot_of(beam)

    @pl.when(beam % CHILD == 0)
    def _():
        for kv in range(kv_heads):
            keys_ref[kv] = split_keys(parent_buf[slot, :tokens, kv_lanes(kv)])
        for pair in range(pairs):
            sums_ref[pair] = dot_first(
                parent_buf[slot, tokens:, kv_lanes(pair // pairs_kv)],
                one_hot_rows(sum_rows, sum_rows // 2, 2 * (pair % pairs_kv)),
            )

    stack_queries(query_ref, stacked_ref, pairs)
    total = jnp.zeros((1, tokens), jnp.float32)
    lowest = jnp.full((1, LANES_BOTH), SAFE_HIGH, jnp.float32)
    highest = jnp.full((1, LANES_BOTH), SAFE_LOW, jnp.float32)
    for pair in range(pairs):
        top, bottom = plain_block(
            keys_ref[pair // pairs_kv], stacked_ref[pair], sums_ref[pair]
        )
        top = jnp.sum(top + state_ref[0, 0, pair], axis=0, keepdims=True)
        bottom = jnp.sum(bottom + state_ref[0, 1, pair], axis=0, keepdims=True)
        lowest = jnp.minimum(lowest, bottom)
        highest = jnp.maximum(highest, bottom)
        ratio = top / bottom
        total = total + ratio[:, :tokens] + ratio[:, tokens:]
    reward_ref[pl.ds(beam, 1), :] = total

    @pl.when(beam == 0)
    def _():
        range_ref[0:1] = lowest
        range_ref[1:2] = highest

    @pl.when(beam > 0)
    def _():
        range_ref[0:1] = jnp.minimum(range_ref[0:1], lowest)
        range_ref[1:2] = jnp.maximum(range_ref[1:2], highest)

    def fetch(source, target):
        copy = pltpu.make_async_copy(source, target, slow_sem)
        copy.start()
        copy.wait()

    def online_step(pair, keys, sums, allowed=None):
        scores = dot_last(keys, slow_query_pair(pair))
        if allowed is not None:
            scores = jnp.where(allowed, scores, MASKED)
        scores = scores.reshape(-1, 8, LANES_BOTH)
        before = slow_state[0, pair]
        after = jnp.maximum(before, jnp.max(scores, axis=0))
        fade = jnp.exp2((before - after) * LOG2_SCALE)
        weights = jnp.exp2((scores - after[None]) * LOG2_SCALE)
        sums = sums.reshape(weights.shape)
        slow_state[0, pair] = after
        slow_state[1, pair] = slow_state[1, pair] * fade + jnp.sum(weights * sums, axis=0)
        slow_state[2, pair] = slow_state[2, pair] * fade + jnp.sum(weights, axis=0)

    def slow_query_pair(pair):
        start = pl.multiple_of(pair * LANES_BOTH, LANES_BOTH)
        return jnp.concatenate(
            [
                slow_query[:, pl.ds(start, HEAD_SIZE)],
                slow_query[:, pl.ds(start + HEAD_SIZE, HEAD_SIZE)],
            ],
            axis=0,
        )

    def slow_lanes(pair):
        return pl.ds(pl.multiple_of(pair // pairs_kv * HEAD_SIZE, HEAD_SIZE), HEAD_SIZE)

    def slow_plain(pair, allowed=None):
        spread = dot_first(weight_ref[...], one_hot_rows(heads, heads, 2 * pair))
        sums = jnp.dot(
            slow_block[1, :, slow_lanes(pair)],
            spread.astype(jnp.bfloat16),
            preferred_element_type=jnp.float32,
        )
        online_step(pair, slow_block[0, :, slow_lanes(pair)], sums, allowed)

    def slow_beam(b):
        fetch(query_any.at[b], slow_query)
        slow_state[0] = jnp.full(slow_state.shape[1:], MASKED, jnp.float32)
        slow_state[1] = jnp.zeros(slow_state.shape[1:], jnp.float32)
        slow_state[2] = jnp.zeros(slow_state.shape[1:], jnp.float32)

        @pl.loop(0, live_count[b])
        def _(i):
            fetch(store_any.at[block_ids[b, i] - own * blocks], slow_block)
            pl.loop(0, pairs)(lambda pair: slow_plain(pair))

        fetch(new_any.at[b], slow_block)
        pl.loop(0, pairs)(lambda pair: slow_plain(pair, causal(tokens)))
        here = slot_of(b)
        reward_ref[pl.ds(b, 1), :] = jnp.zeros((1, tokens), jnp.float32)

        @pl.loop(0, pairs)
        def _(pair):
            sums = dot_first(
                parent_buf[here, tokens:, slow_lanes(pair)],
                one_hot_rows(sum_rows, sum_rows // 2, 2 * (pair % pairs_kv)),
            )
            online_step(pair, parent_buf[here, :tokens, slow_lanes(pair)], sums)
            state = slow_state[0, pair]
            row_max = jnp.max(state, axis=0, keepdims=True)
            fade = jnp.exp2((state - row_max) * LOG2_SCALE)
            ratio = jnp.sum(slow_state[1, pair] * fade, axis=0, keepdims=True) / jnp.sum(
                slow_state[2, pair] * fade, axis=0, keepdims=True
            )
            reward_ref[pl.ds(b, 1), :] += ratio[:, :tokens] + ratio[:, tokens:]

    @pl.when(beam == beams - 1)
    def _():
        @pl.loop(0, keep_dev)
        def _(j):
            for copy in kept_stores(j, 0):
                copy.wait()

        low_ok = jnp.min(range_ref[0:1]) >= SAFE_LOW
        high_ok = jnp.max(range_ref[1:2]) <= SAFE_HIGH

        @pl.when(jnp.logical_not(low_ok & high_ok))
        def _():
            pl.loop(0, beams)(slow_beam)


def on_device(
    queries,
    new_kv,
    newest_key_value,
    ancestor_block_store,
    parent,
    ancestors,
    ancestor_count,
    keep_list,
    w_reward,
):
    devices = lax.axis_size("beam")
    mp = lax.axis_size("mp")
    own = lax.axis_index("beam").reshape(1)
    beam_dev, _, tokens, kv_width = new_kv.shape
    q_width = queries.shape[2]
    heads = q_width // HEAD_SIZE
    kv_heads = kv_width // HEAD_SIZE
    per_group = heads // kv_heads
    pairs = heads // 2
    pairs_kv = pairs // kv_heads
    keep_dev = keep_list.shape[0] // devices
    blocks = ancestor_block_store.shape[0]
    pack_rows = 3 * tokens + 2 * per_group
    packed = jax.ShapeDtypeStruct((pack_rows, kv_width), new_kv.dtype)
    weight = w_reward.reshape(heads, HEAD_SIZE)
    weight_spec = pl.BlockSpec((heads, HEAD_SIZE), lambda i, *_: (0, 0))
    dma = pltpu.SemaphoreType.DMA

    sent = pl.pallas_call(
        functools.partial(pack_kernel, beam_dev=beam_dev, keep_dev=keep_dev),
        out_shape=(packed,) * devices,
        grid_spec=pltpu.PrefetchScalarGridSpec(
            num_scalar_prefetch=3,
            grid=(1,),
            in_specs=[weight_spec, ANY, ANY],
            out_specs=(ANY,) * devices,
            scratch_shapes=[
                pltpu.VMEM((devices, pack_rows, kv_width), jnp.bfloat16),
                pltpu.VMEM((devices, tokens, kv_width), jnp.bfloat16),
                dma((devices,)),
                dma((devices, 3)),
                dma((devices,)),
            ],
        ),
        name="pack",
    )(own, parent, keep_list, weight, newest_key_value, new_kv)

    arrived = [sent[0]] + [None] * (devices - 1)
    for k in range(devices - 1, 0, -1):
        arrived[k] = lax.ppermute(sent[k], "beam", [(i, i ^ k) for i in range(devices)])

    query_spec = pl.BlockSpec((1, tokens, q_width), lambda b, *_: (b, 0, 0))
    state_shape = (beam_dev, 2, pairs, 8, LANES_BOTH)
    state_spec = pl.BlockSpec((1,) + state_shape[1:], lambda b, *_: (b, 0, 0, 0, 0))
    state = pl.pallas_call(
        functools.partial(local_kernel, pairs=pairs, pairs_kv=pairs_kv),
        out_shape=jax.ShapeDtypeStruct(state_shape, jnp.float32),
        grid_spec=pltpu.PrefetchScalarGridSpec(
            num_scalar_prefetch=3,
            grid=(beam_dev,),
            in_specs=[
                query_spec,
                pl.BlockSpec((1, 2, tokens, kv_width), lambda b, *_: (b, 0, 0, 0)),
                pl.BlockSpec(
                    ancestor_block_store.shape,
                    lambda b, *_: (0, 0, 0, 0),
                    pipeline_mode=pl.Buffered(1),
                ),
                weight_spec,
            ],
            out_specs=state_spec,
            scratch_shapes=[
                pltpu.VMEM((pairs, HEAD_SIZE, LANES_BOTH), jnp.bfloat16),
                pltpu.VMEM((blocks, kv_heads, tokens, LANES_BOTH), jnp.bfloat16),
                pltpu.VMEM((blocks, pairs, tokens, LANES_BOTH), jnp.float32),
                pltpu.VMEM((pairs, LANES_BOTH, HEAD_SIZE), jnp.bfloat16),
            ],
        ),
        cost_estimate=pl.CostEstimate(
            flops=20_000_000_000, transcendentals=20_000_000, bytes_accessed=16_000_000
        ),
        name="local",
    )(own, ancestors, ancestor_count, queries, new_kv, ancestor_block_store, weight)

    partial_reward, kept_blocks = pl.pallas_call(
        functools.partial(
            parent_kernel, devices=devices, pairs=pairs, pairs_kv=pairs_kv
        ),
        out_shape=(
            jax.ShapeDtypeStruct((beam_dev, tokens), jnp.float32),
            jax.ShapeDtypeStruct((keep_dev,) + new_kv.shape[1:], new_kv.dtype),
        ),
        grid_spec=pltpu.PrefetchScalarGridSpec(
            num_scalar_prefetch=5,
            grid=(beam_dev,),
            in_specs=[query_spec, state_spec, weight_spec] + [ANY] * (3 + devices),
            out_specs=(
                pl.BlockSpec((beam_dev, tokens), lambda b, *_: (0, 0)),
                ANY,
            ),
            scratch_shapes=[
                pltpu.VMEM((devices, tokens + 2 * per_group, kv_width), jnp.bfloat16),
                pltpu.VMEM((devices, 2 * tokens, kv_width), jnp.bfloat16),
                pltpu.VMEM((kv_heads, tokens, LANES_BOTH), jnp.bfloat16),
                pltpu.VMEM((pairs, tokens, LANES_BOTH), jnp.float32),
                pltpu.VMEM((pairs, LANES_BOTH, HEAD_SIZE), jnp.bfloat16),
                pltpu.VMEM((8, LANES_BOTH), jnp.float32),
                pltpu.VMEM((tokens, q_width), jnp.bfloat16),
                pltpu.VMEM((2, tokens, kv_width), jnp.bfloat16),
                pltpu.VMEM((3, pairs, 8, LANES_BOTH), jnp.float32),
                dma((devices,)),
                dma((devices,)),
                dma((keep_dev, 2)),
                dma(()),
            ],
        ),
        name="parents",
    )(
        own,
        parent,
        keep_list,
        ancestors,
        ancestor_count,
        queries,
        state,
        weight,
        queries,
        new_kv,
        ancestor_block_store,
        *arrived,
    )

    reward = partial_reward
    for shift in range(1, mp):
        ring = [(i, (i + shift) % mp) for i in range(mp)]
        reward = reward + lax.ppermute(partial_reward, "mp", ring)
    return (reward, kept_blocks)


def solution(mesh):
    placed = (
        P("beam", None, "mp"),
        P("beam", None, None, "mp"),
        P("beam", None, None, "mp"),
        P("beam", None, None, "mp"),
        P(),
        P("beam", None),
        P("beam"),
        P(),
        P("mp"),
    )
    return jax.shard_map(
        on_device,
        mesh=mesh,
        in_specs=placed,
        out_specs=(P("beam", None), P("beam", None, None, "mp")),
        check_vma=False,
    )
```

```python
import functools
import math

import jax
import jax.numpy as jnp
from jax import lax
from jax.experimental import pallas as pl
from jax.experimental.pallas import tpu as pltpu
from jax.sharding import PartitionSpec as P

HEAD_SIZE = 128
CHILD = 2
LOG2_SCALE = HEAD_SIZE ** (-0.5) * math.log2(math.e)
MASKED = -1e30
SAFE_LOW = 2.0**-60
SAFE_HIGH = 2.0**100
LANES_BOTH = 2 * HEAD_SIZE
AHEAD = 4
ANY = pl.BlockSpec(memory_space=pl.ANY)


def dot_last(a, b):
    return lax.dot_general(
        a, b, (((1,), (1,)), ((), ())), preferred_element_type=jnp.float32
    )


def dot_first(a, b):
    return lax.dot_general(
        a, b, (((0,), (0,)), ((), ())), preferred_element_type=jnp.float32
    )


def one_hot_rows(rows, period, first):
    shape = (rows, LANES_BOTH)
    row = lax.broadcasted_iota(jnp.int32, shape, 0) % period
    head = first + lax.broadcasted_iota(jnp.int32, shape, 1) // HEAD_SIZE
    return jnp.where(row == head, 1.0, 0.0).astype(jnp.bfloat16)


def split_keys(keys):
    scaled = keys.astype(jnp.float32) * LOG2_SCALE
    high = scaled.astype(jnp.bfloat16)
    low = (scaled - high.astype(jnp.float32)).astype(jnp.bfloat16)
    return jnp.concatenate([high, low], axis=1)


def kv_lanes(kv):
    return slice(kv * HEAD_SIZE, (kv + 1) * HEAD_SIZE)


def query_pair(query, beam, pair):
    start = pair * LANES_BOTH
    return jnp.concatenate(
        [
            query[beam, :, start : start + HEAD_SIZE],
            query[beam, :, start + HEAD_SIZE : start + LANES_BOTH],
        ],
        axis=0,
    )


def weigh(scores, sums):
    weights = jnp.exp2(scores).reshape(-1, 8, LANES_BOTH)
    return (
        jnp.sum(weights * sums.reshape(weights.shape), axis=0),
        jnp.sum(weights, axis=0),
    )


def row_sum(x):
    return jnp.sum(x, axis=0, keepdims=True)


def causal(tokens):
    shape = (tokens, LANES_BOTH)
    key_pos = lax.broadcasted_iota(jnp.int32, shape, 0)
    token_pos = lax.broadcasted_iota(jnp.int32, shape, 1) % tokens
    return key_pos <= token_pos


def find_row(table, start, step, count, first, beam_dev):
    found = jnp.int32(0)
    for i in range(count):
        row = table[start + i * step] - first
        found = jnp.where((row >= 0) & (row < beam_dev), row, found)
    return found


def pack_kernel(own_ref, parent_ref, keep_ref, weight_ref, newest_ref, new_ref, *rest, beam_dev, keep_dev):
    devices = len(rest) - 5
    outs = rest[:devices]
    pack_buf, value_buf, value_sem, rest_sem, out_sem = rest[devices:]
    groups = beam_dev // CHILD
    own = own_ref[0]
    tokens = newest_ref.shape[2]
    kv_heads = newest_ref.shape[3] // HEAD_SIZE
    per_group = weight_ref.shape[0] // kv_heads

    def loads(k, row, kept):
        return (
            pltpu.make_async_copy(
                newest_ref.at[row, 0],
                pack_buf.at[k, pl.ds(2 * tokens, tokens)],
                rest_sem.at[k, 0],
            ),
            pltpu.make_async_copy(
                new_ref.at[kept, 0], pack_buf.at[k, pl.ds(0, tokens)], rest_sem.at[k, 1]
            ),
            pltpu.make_async_copy(
                new_ref.at[kept, 1],
                pack_buf.at[k, pl.ds(tokens, tokens)],
                rest_sem.at[k, 2],
            ),
            pltpu.make_async_copy(
                newest_ref.at[row, 1], value_buf.at[k], value_sem.at[k]
            ),
        )

    @pl.loop(0, devices)
    def _(k):
        peer = own ^ k
        row = find_row(parent_ref, peer * beam_dev, CHILD, groups, own * beam_dev, beam_dev)
        kept = find_row(keep_ref, peer * keep_dev, 1, keep_dev, own * beam_dev, beam_dev)
        for copy in loads(k, row, kept):
            copy.start()

    for k in range(devices - 1, -1, -1):
        for copy in loads(k, 0, 0):
            copy.wait()
        for kv in range(kv_heads):
            total = dot_last(
                weight_ref[kv * per_group : (kv + 1) * per_group],
                value_buf[k, :, kv_lanes(kv)],
            )
            high = total.astype(jnp.bfloat16)
            low = (total - high.astype(jnp.float32)).astype(jnp.bfloat16)
            pack_buf[k, 3 * tokens : 3 * tokens + per_group, kv_lanes(kv)] = high
            pack_buf[k, 3 * tokens + per_group :, kv_lanes(kv)] = low
        pltpu.make_async_copy(pack_buf.at[k], outs[k], out_sem.at[k]).start()
    for k in range(devices):
        pltpu.make_async_copy(pack_buf.at[k], outs[k], out_sem.at[k]).wait()


def local_kernel(
    own_ref,
    block_ids,
    live_count,
    query_any,
    new_any,
    store_any,
    weight_ref,
    state_ref,
    query_buf,
    new_buf,
    store_buf,
    spread_ref,
    keys_ref,
    sums_ref,
    query_sem,
    new_sem,
    store_sem,
    *,
    pairs,
    pairs_kv,
    slots,
):
    beams, tokens = query_buf.shape[:2]
    blocks = store_buf.shape[1]
    heads = weight_ref.shape[0]
    kv_heads = pairs // pairs_kv
    depth = min(AHEAD, beams)

    def store_copies():
        return [
            pltpu.make_async_copy(
                store_any.at[:, side], store_buf.at[side], store_sem.at[side]
            )
            for side in (1, 0)
        ]

    def beam_copies(b):
        return (
            pltpu.make_async_copy(query_any.at[b], query_buf.at[b], query_sem.at[b]),
            pltpu.make_async_copy(new_any.at[b], new_buf.at[b], new_sem.at[b]),
        )

    for copy in store_copies():
        copy.start()
    for pair in range(pairs):
        spread_ref[pair] = dot_first(
            weight_ref[...], one_hot_rows(heads, heads, 2 * pair)
        ).astype(jnp.bfloat16)
    for copy in store_copies():
        copy.wait()
    for b in range(depth):
        for copy in beam_copies(b):
            copy.start()
    for pair in range(pairs):
        values = store_buf[1, :, :, kv_lanes(pair // pairs_kv)]
        sums_ref[pair] = jnp.dot(
            values.reshape(blocks * tokens, HEAD_SIZE),
            spread_ref[pair],
            preferred_element_type=jnp.float32,
        )

    @pl.loop(0, blocks)
    def _(block):
        for kv in range(kv_heads):
            keys_ref[block, kv] = split_keys(store_buf[0, block, :, kv_lanes(kv)])

    allowed = causal(tokens)

    def beam_body(b, count):
        ids = [block_ids[b, i] - own_ref[0] * blocks for i in range(count)]
        for kv in range(kv_heads):
            keys = [keys_ref[i, kv] for i in ids]
            keys = jnp.concatenate(
                keys + [split_keys(new_buf[b, 0, :, kv_lanes(kv)])], axis=0
            )
            for pair in range(kv * pairs_kv, (kv + 1) * pairs_kv):
                own_sums = jnp.dot(
                    new_buf[b, 1, :, kv_lanes(kv)],
                    spread_ref[pair],
                    preferred_element_type=jnp.float32,
                )
                query = query_pair(query_buf, b, pair)
                scores = dot_last(keys, jnp.concatenate([query, query], axis=1))
                own_scores = jnp.where(allowed, scores[count * tokens :], MASKED)
                top, bottom = weigh(own_scores, own_sums)
                for i, block in enumerate(ids):
                    sums = sums_ref[pair, pl.ds(pl.multiple_of(block * tokens, tokens), tokens)]
                    more = weigh(scores[i * tokens : (i + 1) * tokens], sums)
                    top, bottom = top + more[0], bottom + more[1]
                state_ref[b, 0, pair : pair + 1] = row_sum(top)
                state_ref[b, 1, pair : pair + 1] = row_sum(bottom)

    @pl.loop(0, beams)
    def _(b):
        @pl.when(b + depth < beams)
        def _():
            for copy in beam_copies(b + depth):
                copy.start()

        for copy in beam_copies(b):
            copy.wait()
        for count in range(1, slots + 1):

            @pl.when(live_count[b] == count)
            def _():
                beam_body(b, count)


def parent_kernel(own_ref, parent_ref, keep_ref, block_ids, live_count, *rest, devices, pairs, pairs_kv):
    state_ref, weight_ref, query_any, new_any, store_any = rest[:5]
    arrived = rest[5 : 5 + devices]
    reward_ref, kept_ref = rest[5 + devices : 7 + devices]
    (
        query_buf,
        parent_buf,
        kept_buf,
        slow_block,
        slow_state,
        query_sem,
        parent_sem,
        load_sem,
        store_sem,
        slow_sem,
    ) = rest[7 + devices :]
    beams, tokens = query_buf.shape[:2]
    own = own_ref[0]
    keep_dev = kept_ref.shape[0]
    kv_heads = pairs // pairs_kv
    blocks = store_any.shape[0]
    sum_rows = parent_buf.shape[1] - tokens
    heads = 2 * pairs
    depth = min(AHEAD, beams)

    def query_load(b):
        return pltpu.make_async_copy(query_any.at[b], query_buf.at[b], query_sem.at[b])

    def parent_load(k):
        return pltpu.make_async_copy(
            arrived[k].at[pl.ds(2 * tokens, tokens + sum_rows)],
            parent_buf.at[k],
            parent_sem.at[k],
        )

    def kept_load(k):
        return pltpu.make_async_copy(
            arrived[k].at[pl.ds(0, 2 * tokens)], kept_buf.at[k], load_sem.at[k]
        )

    def kept_stores(j, k):
        return [
            pltpu.make_async_copy(
                kept_buf.at[k, pl.ds(side * tokens, tokens)],
                kept_ref.at[j, side],
                store_sem.at[j, side],
            )
            for side in range(2)
        ]

    def slot_of(b):
        return (parent_ref[own * beams + b] // beams) ^ own

    for k in range(devices):
        parent_load(k).start()
    for b in range(depth):
        query_load(b).start()
    for k in range(devices):
        kept_load(k).start()
    for k in range(devices):
        parent_load(k).wait()

    def group_step(group, limits):
        slot = slot_of(group * CHILD)
        lowest, highest = limits
        for child in range(CHILD):
            b = group * CHILD + child

            @pl.when(b + depth < beams)
            def _():
                query_load(b + depth).start()

            query_load(b).wait()
        totals = [jnp.zeros((1, tokens), jnp.float32) for _ in range(CHILD)]
        for kv in range(kv_heads):
            keys = split_keys(parent_buf[slot, :tokens, kv_lanes(kv)])
            rows = parent_buf[slot, tokens:, kv_lanes(kv)]
            for pair in range(kv * pairs_kv, (kv + 1) * pairs_kv):
                hot = one_hot_rows(sum_rows, sum_rows // 2, 2 * (pair % pairs_kv))
                sums = dot_first(rows, hot)
                for child in range(CHILD):
                    b = group * CHILD + child
                    query = query_pair(query_buf, b, pair)
                    scores = dot_last(keys, jnp.concatenate([query, query], axis=1))
                    top, bottom = weigh(scores, sums)
                    top = row_sum(top) + state_ref[b, 0, pair : pair + 1]
                    bottom = row_sum(bottom) + state_ref[b, 1, pair : pair + 1]
                    lowest = jnp.minimum(lowest, bottom)
                    highest = jnp.maximum(highest, bottom)
                    ratio = top / bottom
                    totals[child] += ratio[:, :tokens] + ratio[:, tokens:]
        for child in range(CHILD):
            reward_ref[pl.ds(group * CHILD + child, 1), :] = totals[child]
        return lowest, highest

    def start_kept():
        for k in range(devices):
            kept_load(k).wait()

        @pl.loop(0, keep_dev)
        def _(j):
            k = (keep_ref[own * keep_dev + j] // beams) ^ own
            for copy in kept_stores(j, k):
                copy.start()

    limits = (
        jnp.full((1, LANES_BOTH), SAFE_HIGH, jnp.float32),
        jnp.full((1, LANES_BOTH), SAFE_LOW, jnp.float32),
    )
    groups = beams // CHILD
    limits = lax.fori_loop(0, groups // 2, group_step, limits)
    start_kept()
    lowest, highest = lax.fori_loop(groups // 2, groups, group_step, limits)

    @pl.loop(0, keep_dev)
    def _(j):
        for copy in kept_stores(j, 0):
            copy.wait()

    def fetch(source, target):
        copy = pltpu.make_async_copy(source, target, slow_sem)
        copy.start()
        copy.wait()

    def online_step(b, pair, keys, sums, allowed=None):
        start = pl.multiple_of(pair * LANES_BOTH, LANES_BOTH)
        query = jnp.concatenate(
            [
                query_buf[b, :, pl.ds(start, HEAD_SIZE)],
                query_buf[b, :, pl.ds(start + HEAD_SIZE, HEAD_SIZE)],
            ],
            axis=0,
        )
        scores = dot_last(keys, query)
        if allowed is not None:
            scores = jnp.where(allowed, scores, MASKED)
        scores = scores.reshape(-1, 8, LANES_BOTH)
        before = slow_state[0, pair]
        after = jnp.maximum(before, jnp.max(scores, axis=0))
        fade = jnp.exp2((before - after) * LOG2_SCALE)
        weights = jnp.exp2((scores - after[None]) * LOG2_SCALE)
        sums = sums.reshape(weights.shape)
        slow_state[0, pair] = after
        slow_state[1, pair] = slow_state[1, pair] * fade + jnp.sum(weights * sums, axis=0)
        slow_state[2, pair] = slow_state[2, pair] * fade + jnp.sum(weights, axis=0)

    def slow_lanes(pair):
        return pl.ds(pl.multiple_of(pair // pairs_kv * HEAD_SIZE, HEAD_SIZE), HEAD_SIZE)

    def slow_plain(b, pair, allowed=None):
        spread = dot_first(weight_ref[...], one_hot_rows(heads, heads, 2 * pair))
        sums = jnp.dot(
            slow_block[1, :, slow_lanes(pair)],
            spread.astype(jnp.bfloat16),
            preferred_element_type=jnp.float32,
        )
        online_step(b, pair, slow_block[0, :, slow_lanes(pair)], sums, allowed)

    def slow_beam(b):
        slow_state[0] = jnp.full(slow_state.shape[1:], MASKED, jnp.float32)
        slow_state[1] = jnp.zeros(slow_state.shape[1:], jnp.float32)
        slow_state[2] = jnp.zeros(slow_state.shape[1:], jnp.float32)

        @pl.loop(0, live_count[b])
        def _(i):
            fetch(store_any.at[block_ids[b, i] - own * blocks], slow_block)
            pl.loop(0, pairs)(lambda pair: slow_plain(b, pair))

        fetch(new_any.at[b], slow_block)
        pl.loop(0, pairs)(lambda pair: slow_plain(b, pair, causal(tokens)))
        here = slot_of(b)
        reward_ref[pl.ds(b, 1), :] = jnp.zeros((1, tokens), jnp.float32)

        @pl.loop(0, pairs)
        def _(pair):
            sums = dot_first(
                parent_buf[here, tokens:, slow_lanes(pair)],
                one_hot_rows(sum_rows, sum_rows // 2, 2 * (pair % pairs_kv)),
            )
            online_step(b, pair, parent_buf[here, :tokens, slow_lanes(pair)], sums)
            state = slow_state[0, pair]
            row_max = jnp.max(state, axis=0, keepdims=True)
            fade = jnp.exp2((state - row_max) * LOG2_SCALE)
            ratio = jnp.sum(slow_state[1, pair] * fade, axis=0, keepdims=True) / jnp.sum(
                slow_state[2, pair] * fade, axis=0, keepdims=True
            )
            reward_ref[pl.ds(b, 1), :] += ratio[:, :tokens] + ratio[:, tokens:]

    low_ok = jnp.min(lowest) >= SAFE_LOW
    high_ok = jnp.max(highest) <= SAFE_HIGH

    @pl.when(jnp.logical_not(low_ok & high_ok))
    def _():
        pl.loop(0, beams)(slow_beam)


def on_device(
    queries,
    new_kv,
    newest_key_value,
    ancestor_block_store,
    parent,
    ancestors,
    ancestor_count,
    keep_list,
    w_reward,
):
    devices = lax.axis_size("beam")
    mp = lax.axis_size("mp")
    own = lax.axis_index("beam").reshape(1)
    beam_dev, _, tokens, kv_width = new_kv.shape
    q_width = queries.shape[2]
    heads = q_width // HEAD_SIZE
    kv_heads = kv_width // HEAD_SIZE
    per_group = heads // kv_heads
    pairs = heads // 2
    pairs_kv = pairs // kv_heads
    keep_dev = keep_list.shape[0] // devices
    blocks = ancestor_block_store.shape[0]
    pack_rows = 3 * tokens + 2 * per_group
    packed = jax.ShapeDtypeStruct((pack_rows, kv_width), new_kv.dtype)
    weight = w_reward.reshape(heads, HEAD_SIZE)
    weight_spec = pl.BlockSpec((heads, HEAD_SIZE), lambda i, *_: (0, 0))
    dma = pltpu.SemaphoreType.DMA

    sent = pl.pallas_call(
        functools.partial(pack_kernel, beam_dev=beam_dev, keep_dev=keep_dev),
        out_shape=(packed,) * devices,
        grid_spec=pltpu.PrefetchScalarGridSpec(
            num_scalar_prefetch=3,
            grid=(1,),
            in_specs=[weight_spec, ANY, ANY],
            out_specs=(ANY,) * devices,
            scratch_shapes=[
                pltpu.VMEM((devices, pack_rows, kv_width), jnp.bfloat16),
                pltpu.VMEM((devices, tokens, kv_width), jnp.bfloat16),
                dma((devices,)),
                dma((devices, 3)),
                dma((devices,)),
            ],
        ),
        name="pack",
    )(own, parent, keep_list, weight, newest_key_value, new_kv)

    arrived = [sent[0]] + [None] * (devices - 1)
    for k in range(devices - 1, 0, -1):
        arrived[k] = lax.ppermute(sent[k], "beam", [(i, i ^ k) for i in range(devices)])

    state_shape = (beam_dev, 2, pairs, LANES_BOTH)
    state_spec = pl.BlockSpec(state_shape, lambda i, *_: (0, 0, 0, 0))
    state = pl.pallas_call(
        functools.partial(
            local_kernel, pairs=pairs, pairs_kv=pairs_kv, slots=ancestors.shape[1]
        ),
        out_shape=jax.ShapeDtypeStruct(state_shape, jnp.float32),
        grid_spec=pltpu.PrefetchScalarGridSpec(
            num_scalar_prefetch=3,
            grid=(1,),
            in_specs=[ANY, ANY, ANY, weight_spec],
            out_specs=state_spec,
            scratch_shapes=[
                pltpu.VMEM(queries.shape, jnp.bfloat16),
                pltpu.VMEM(new_kv.shape, jnp.bfloat16),
                pltpu.VMEM((2, blocks, tokens, kv_width), jnp.bfloat16),
                pltpu.VMEM((pairs, HEAD_SIZE, LANES_BOTH), jnp.bfloat16),
                pltpu.VMEM((blocks, kv_heads, tokens, LANES_BOTH), jnp.bfloat16),
                pltpu.VMEM((pairs, blocks * tokens, LANES_BOTH), jnp.float32),
                dma((beam_dev,)),
                dma((beam_dev,)),
                dma((2,)),
            ],
        ),
        cost_estimate=pl.CostEstimate(
            flops=20_000_000_000, transcendentals=20_000_000, bytes_accessed=16_000_000
        ),
        name="local",
    )(own, ancestors, ancestor_count, queries, new_kv, ancestor_block_store, weight)

    partial_reward, kept_blocks = pl.pallas_call(
        functools.partial(
            parent_kernel, devices=devices, pairs=pairs, pairs_kv=pairs_kv
        ),
        out_shape=(
            jax.ShapeDtypeStruct((beam_dev, tokens), jnp.float32),
            jax.ShapeDtypeStruct((keep_dev,) + new_kv.shape[1:], new_kv.dtype),
        ),
        grid_spec=pltpu.PrefetchScalarGridSpec(
            num_scalar_prefetch=5,
            grid=(1,),
            in_specs=[state_spec, weight_spec] + [ANY] * (3 + devices),
            out_specs=(
                pl.BlockSpec((beam_dev, tokens), lambda i, *_: (0, 0)),
                ANY,
            ),
            scratch_shapes=[
                pltpu.VMEM(queries.shape, jnp.bfloat16),
                pltpu.VMEM((devices, tokens + 2 * per_group, kv_width), jnp.bfloat16),
                pltpu.VMEM((devices, 2 * tokens, kv_width), jnp.bfloat16),
                pltpu.VMEM((2, tokens, kv_width), jnp.bfloat16),
                pltpu.VMEM((3, pairs, 8, LANES_BOTH), jnp.float32),
                dma((beam_dev,)),
                dma((devices,)),
                dma((devices,)),
                dma((keep_dev, 2)),
                dma(()),
            ],
        ),
        name="parents",
    )(
        own,
        parent,
        keep_list,
        ancestors,
        ancestor_count,
        state,
        weight,
        queries,
        new_kv,
        ancestor_block_store,
        *arrived,
    )

    reward = partial_reward
    for shift in range(1, mp):
        ring = [(i, i ^ shift) for i in range(mp)]
        reward = reward + lax.ppermute(partial_reward, "mp", ring)
    return (reward, kept_blocks)


def solution(mesh):
    placed = (
        P("beam", None, "mp"),
        P("beam", None, None, "mp"),
        P("beam", None, None, "mp"),
        P("beam", None, None, "mp"),
        P(),
        P("beam", None),
        P("beam"),
        P(),
        P("mp"),
    )
    return jax.shard_map(
        on_device,
        mesh=mesh,
        in_specs=placed,
        out_specs=(P("beam", None), P("beam", None, None, "mp")),
        check_vma=False,
    )
```

```python
import functools
import math

import jax
import jax.numpy as jnp
from jax import lax
from jax.experimental import pallas as pl
from jax.experimental.pallas import tpu as pltpu
from jax.sharding import PartitionSpec as P

HEAD_SIZE = 128
CHILD = 2
LOG2_SCALE = HEAD_SIZE ** (-0.5) * math.log2(math.e)
MASKED = -1e30
SAFE_LOW = 2.0**-60
SAFE_HIGH = 2.0**100
LANES_BOTH = 2 * HEAD_SIZE
AHEAD = 4
ANY = pl.BlockSpec(memory_space=pl.ANY)


def dot_last(a, b):
    return lax.dot_general(
        a, b, (((1,), (1,)), ((), ())), preferred_element_type=jnp.float32
    )


def dot_first(a, b):
    return lax.dot_general(
        a, b, (((0,), (0,)), ((), ())), preferred_element_type=jnp.float32
    )


def one_hot_rows(rows, period, first):
    shape = (rows, LANES_BOTH)
    row = lax.broadcasted_iota(jnp.int32, shape, 0) % period
    head = first + lax.broadcasted_iota(jnp.int32, shape, 1) // HEAD_SIZE
    return jnp.where(row == head, 1.0, 0.0).astype(jnp.bfloat16)


def lane_rows(rows, period):
    shape = (rows, HEAD_SIZE)
    row = lax.broadcasted_iota(jnp.int32, shape, 0) % period
    lane = lax.broadcasted_iota(jnp.int32, shape, 1)
    return jnp.where(row == lane, 1.0, 0.0).astype(jnp.bfloat16)


def spread_columns(columns, first):
    shape = (columns.shape[0], HEAD_SIZE)
    return jnp.concatenate(
        [
            jnp.broadcast_to(columns[:, first : first + 1], shape),
            jnp.broadcast_to(columns[:, first + 1 : first + 2], shape),
        ],
        axis=1,
    )


def split_keys(keys):
    scaled = keys.astype(jnp.float32) * LOG2_SCALE
    high = scaled.astype(jnp.bfloat16)
    low = (scaled - high.astype(jnp.float32)).astype(jnp.bfloat16)
    return jnp.concatenate([high, low], axis=1)


def kv_lanes(kv):
    return slice(kv * HEAD_SIZE, (kv + 1) * HEAD_SIZE)


def query_pair(query, beam, pair):
    start = pair * LANES_BOTH
    return jnp.concatenate(
        [
            query[beam, :, start : start + HEAD_SIZE],
            query[beam, :, start + HEAD_SIZE : start + LANES_BOTH],
        ],
        axis=0,
    )


def weigh(scores, sums):
    weights = jnp.exp2(scores).reshape(-1, 8, LANES_BOTH)
    return (
        jnp.sum(weights * sums.reshape(weights.shape), axis=0),
        jnp.sum(weights, axis=0),
    )


def row_sum(x):
    return jnp.sum(x, axis=0, keepdims=True)


def causal(tokens):
    shape = (tokens, LANES_BOTH)
    key_pos = lax.broadcasted_iota(jnp.int32, shape, 0)
    token_pos = lax.broadcasted_iota(jnp.int32, shape, 1) % tokens
    return key_pos <= token_pos


def find_row(table, start, step, count, first, beam_dev):
    found = jnp.int32(0)
    for i in range(count):
        row = table[start + i * step] - first
        found = jnp.where((row >= 0) & (row < beam_dev), row, found)
    return found


def pack_kernel(own_ref, parent_ref, keep_ref, weight_ref, newest_ref, new_ref, *rest, beam_dev, keep_dev):
    devices = len(rest) - 3
    outs = rest[:devices]
    value_buf, value_sem, rest_sem = rest[devices:]
    groups = beam_dev // CHILD
    first = own_ref[0] * beam_dev
    tokens = newest_ref.shape[2]
    kv_heads = newest_ref.shape[3] // HEAD_SIZE
    per_group = weight_ref.shape[0] // kv_heads

    def loads(k, row, kept):
        out = outs[k]
        return (
            pltpu.make_async_copy(
                newest_ref.at[row, 1], value_buf.at[k], value_sem.at[k]
            ),
            pltpu.make_async_copy(
                newest_ref.at[row, 0],
                out.at[pl.ds(2 * tokens, tokens)],
                rest_sem.at[k, 0],
            ),
            pltpu.make_async_copy(
                new_ref.at[kept, 0], out.at[pl.ds(0, tokens)], rest_sem.at[k, 1]
            ),
            pltpu.make_async_copy(
                new_ref.at[kept, 1], out.at[pl.ds(tokens, tokens)], rest_sem.at[k, 2]
            ),
        )

    for k in range(devices):
        peer = own_ref[0] ^ k
        row = find_row(parent_ref, peer * beam_dev, CHILD, groups, first, beam_dev)
        kept = find_row(keep_ref, peer * keep_dev, 1, keep_dev, first, beam_dev)
        for copy in loads(k, row, kept):
            copy.start()
    for k in range(devices):
        value_copy = loads(k, 0, 0)[0]
        value_copy.wait()
        for kv in range(kv_heads):
            total = dot_last(
                weight_ref[kv * per_group : (kv + 1) * per_group],
                value_buf[k, :, kv_lanes(kv)],
            )
            high = total.astype(jnp.bfloat16)
            low = (total - high.astype(jnp.float32)).astype(jnp.bfloat16)
            outs[k][3 * tokens : 3 * tokens + per_group, kv_lanes(kv)] = high
            outs[k][3 * tokens + per_group :, kv_lanes(kv)] = low
    for k in range(devices):
        for copy in loads(k, 0, 0)[1:]:
            copy.wait()


def local_kernel(
    own_ref,
    block_ids,
    live_count,
    query_any,
    new_any,
    store_any,
    weight_ref,
    state_ref,
    query_buf,
    new_buf,
    store_buf,
    spread_ref,
    keys_ref,
    sums_ref,
    query_sem,
    new_sem,
    store_sem,
    *,
    pairs,
    pairs_kv,
    slots,
):
    beams, tokens = query_buf.shape[:2]
    blocks = store_buf.shape[1]
    heads = weight_ref.shape[0]
    kv_heads = pairs // pairs_kv
    depth = min(AHEAD, beams)

    def store_copies():
        return [
            pltpu.make_async_copy(
                store_any.at[:, side], store_buf.at[side], store_sem.at[side]
            )
            for side in (1, 0)
        ]

    def beam_copies(b):
        return (
            pltpu.make_async_copy(query_any.at[b], query_buf.at[b], query_sem.at[b]),
            pltpu.make_async_copy(new_any.at[b], new_buf.at[b], new_sem.at[b]),
        )

    for copy in store_copies():
        copy.start()
    for pair in range(pairs):
        spread_ref[pair] = dot_first(
            weight_ref[...], one_hot_rows(heads, heads, 2 * pair)
        ).astype(jnp.bfloat16)
    for copy in store_copies():
        copy.wait()
    for b in range(depth):
        for copy in beam_copies(b):
            copy.start()
    for pair in range(pairs):
        values = store_buf[1, :, :, kv_lanes(pair // pairs_kv)]
        sums_ref[pair] = jnp.dot(
            values.reshape(blocks * tokens, HEAD_SIZE),
            spread_ref[pair],
            preferred_element_type=jnp.float32,
        )

    @pl.loop(0, blocks)
    def _(block):
        for kv in range(kv_heads):
            keys_ref[block, kv] = split_keys(store_buf[0, block, :, kv_lanes(kv)])

    allowed = causal(tokens)
    turned = dot_first(weight_ref[...], lane_rows(heads, heads)).astype(jnp.bfloat16)

    def beam_body(b, count):
        ids = [block_ids[i, b] - own_ref[0] * blocks for i in range(count)]
        for kv in range(kv_heads):
            keys = [keys_ref[i, kv] for i in ids]
            keys = jnp.concatenate(
                keys + [split_keys(new_buf[b, 0, :, kv_lanes(kv)])], axis=0
            )
            columns = jnp.dot(
                new_buf[b, 1, :, kv_lanes(kv)], turned, preferred_element_type=jnp.float32
            )
            for pair in range(kv * pairs_kv, (kv + 1) * pairs_kv):
                own_sums = spread_columns(columns, 2 * pair)
                query = query_pair(query_buf, b, pair)
                scores = dot_last(keys, jnp.concatenate([query, query], axis=1))
                own_scores = jnp.where(allowed, scores[count * tokens :], MASKED)
                top, bottom = weigh(own_scores, own_sums)
                for i, block in enumerate(ids):
                    sums = sums_ref[pair, pl.ds(pl.multiple_of(block * tokens, tokens), tokens)]
                    more = weigh(scores[i * tokens : (i + 1) * tokens], sums)
                    top, bottom = top + more[0], bottom + more[1]
                state_ref[b, 0, pair : pair + 1] = row_sum(top)
                state_ref[b, 1, pair : pair + 1] = row_sum(bottom)

    @pl.loop(0, beams)
    def _(b):
        @pl.when(b + depth < beams)
        def _():
            for copy in beam_copies(b + depth):
                copy.start()

        for copy in beam_copies(b):
            copy.wait()
        for count in range(1, slots + 1):

            @pl.when(live_count[b] == count)
            def _():
                beam_body(b, count)


def parent_kernel(own_ref, parent_ref, keep_ref, block_ids, live_count, *rest, devices, pairs, pairs_kv):
    state_ref, weight_ref, query_any, new_any, store_any = rest[:5]
    arrived = rest[5 : 5 + devices]
    reward_ref, kept_ref = rest[5 + devices : 7 + devices]
    (
        query_buf,
        parent_buf,
        kept_buf,
        slow_block,
        slow_state,
        query_sem,
        parent_sem,
        load_sem,
        store_sem,
        slow_sem,
    ) = rest[7 + devices :]
    beams, tokens = query_buf.shape[:2]
    own = own_ref[0]
    keep_dev = kept_ref.shape[0]
    kv_heads = pairs // pairs_kv
    blocks = store_any.shape[0]
    sum_rows = parent_buf.shape[1] - tokens
    heads = 2 * pairs
    depth = min(AHEAD, beams)

    def query_load(b):
        return pltpu.make_async_copy(query_any.at[b], query_buf.at[b], query_sem.at[b])

    def parent_load(k):
        return pltpu.make_async_copy(
            arrived[k].at[pl.ds(2 * tokens, tokens + sum_rows)],
            parent_buf.at[k],
            parent_sem.at[k],
        )

    def kept_load(k):
        return pltpu.make_async_copy(
            arrived[k].at[pl.ds(0, 2 * tokens)], kept_buf.at[k], load_sem.at[k]
        )

    def kept_stores(j, k):
        return [
            pltpu.make_async_copy(
                kept_buf.at[k, pl.ds(side * tokens, tokens)],
                kept_ref.at[j, side],
                store_sem.at[j, side],
            )
            for side in range(2)
        ]

    def slot_of(b):
        return (parent_ref[own * beams + b] // beams) ^ own

    for k in range(devices):
        parent_load(k).start()
    for b in range(depth):
        query_load(b).start()
    for k in range(devices):
        kept_load(k).start()
    for k in range(devices):
        parent_load(k).wait()

    def group_step(group, limits):
        slot = slot_of(group * CHILD)
        lowest, highest = limits
        for child in range(CHILD):
            b = group * CHILD + child

            @pl.when(b + depth < beams)
            def _():
                query_load(b + depth).start()

            query_load(b).wait()
        totals = [jnp.zeros((1, tokens), jnp.float32) for _ in range(CHILD)]
        for kv in range(kv_heads):
            keys = parent_buf[slot, :tokens, kv_lanes(kv)]
            columns = dot_first(
                parent_buf[slot, tokens:, kv_lanes(kv)],
                lane_rows(sum_rows, sum_rows // 2),
            )
            for pair in range(kv * pairs_kv, (kv + 1) * pairs_kv):
                sums = spread_columns(columns, 2 * (pair % pairs_kv))
                for child in range(CHILD):
                    b = group * CHILD + child
                    query = query_pair(query_buf, b, pair)
                    scores = dot_last(keys, query) * LOG2_SCALE
                    top, bottom = weigh(scores, sums)
                    top = row_sum(top) + state_ref[b, 0, pair : pair + 1]
                    bottom = row_sum(bottom) + state_ref[b, 1, pair : pair + 1]
                    lowest = jnp.minimum(lowest, bottom)
                    highest = jnp.maximum(highest, bottom)
                    ratio = top / bottom
                    totals[child] += ratio[:, :tokens] + ratio[:, tokens:]
        for child in range(CHILD):
            reward_ref[pl.ds(group * CHILD + child, 1), :] = totals[child]
        return lowest, highest

    def start_kept():
        for k in range(devices):
            kept_load(k).wait()

        @pl.loop(0, keep_dev)
        def _(j):
            k = (keep_ref[own * keep_dev + j] // beams) ^ own
            for copy in kept_stores(j, k):
                copy.start()

    limits = (
        jnp.full((1, LANES_BOTH), SAFE_HIGH, jnp.float32),
        jnp.full((1, LANES_BOTH), SAFE_LOW, jnp.float32),
    )
    groups = beams // CHILD
    limits = lax.fori_loop(0, groups // 2, group_step, limits)
    start_kept()
    lowest, highest = lax.fori_loop(groups // 2, groups, group_step, limits)

    @pl.loop(0, keep_dev)
    def _(j):
        for copy in kept_stores(j, 0):
            copy.wait()

    def fetch(source, target):
        copy = pltpu.make_async_copy(source, target, slow_sem)
        copy.start()
        copy.wait()

    def online_step(b, pair, keys, sums, allowed=None):
        start = pl.multiple_of(pair * LANES_BOTH, LANES_BOTH)
        query = jnp.concatenate(
            [
                query_buf[b, :, pl.ds(start, HEAD_SIZE)],
                query_buf[b, :, pl.ds(start + HEAD_SIZE, HEAD_SIZE)],
            ],
            axis=0,
        )
        scores = dot_last(keys, query)
        if allowed is not None:
            scores = jnp.where(allowed, scores, MASKED)
        scores = scores.reshape(-1, 8, LANES_BOTH)
        before = slow_state[0, pair]
        after = jnp.maximum(before, jnp.max(scores, axis=0))
        fade = jnp.exp2((before - after) * LOG2_SCALE)
        weights = jnp.exp2((scores - after[None]) * LOG2_SCALE)
        sums = sums.reshape(weights.shape)
        slow_state[0, pair] = after
        slow_state[1, pair] = slow_state[1, pair] * fade + jnp.sum(weights * sums, axis=0)
        slow_state[2, pair] = slow_state[2, pair] * fade + jnp.sum(weights, axis=0)

    def slow_lanes(pair):
        return pl.ds(pl.multiple_of(pair // pairs_kv * HEAD_SIZE, HEAD_SIZE), HEAD_SIZE)

    def slow_plain(b, pair, allowed=None):
        spread = dot_first(weight_ref[...], one_hot_rows(heads, heads, 2 * pair))
        sums = jnp.dot(
            slow_block[1, :, slow_lanes(pair)],
            spread.astype(jnp.bfloat16),
            preferred_element_type=jnp.float32,
        )
        online_step(b, pair, slow_block[0, :, slow_lanes(pair)], sums, allowed)

    def slow_beam(b):
        slow_state[0] = jnp.full(slow_state.shape[1:], MASKED, jnp.float32)
        slow_state[1] = jnp.zeros(slow_state.shape[1:], jnp.float32)
        slow_state[2] = jnp.zeros(slow_state.shape[1:], jnp.float32)

        @pl.loop(0, live_count[b])
        def _(i):
            fetch(store_any.at[block_ids[i, b] - own * blocks], slow_block)
            pl.loop(0, pairs)(lambda pair: slow_plain(b, pair))

        fetch(new_any.at[b], slow_block)
        pl.loop(0, pairs)(lambda pair: slow_plain(b, pair, causal(tokens)))
        here = slot_of(b)
        reward_ref[pl.ds(b, 1), :] = jnp.zeros((1, tokens), jnp.float32)

        @pl.loop(0, pairs)
        def _(pair):
            sums = dot_first(
                parent_buf[here, tokens:, slow_lanes(pair)],
                one_hot_rows(sum_rows, sum_rows // 2, 2 * (pair % pairs_kv)),
            )
            online_step(b, pair, parent_buf[here, :tokens, slow_lanes(pair)], sums)
            state = slow_state[0, pair]
            row_max = jnp.max(state, axis=0, keepdims=True)
            fade = jnp.exp2((state - row_max) * LOG2_SCALE)
            ratio = jnp.sum(slow_state[1, pair] * fade, axis=0, keepdims=True) / jnp.sum(
                slow_state[2, pair] * fade, axis=0, keepdims=True
            )
            reward_ref[pl.ds(b, 1), :] += ratio[:, :tokens] + ratio[:, tokens:]

    low_ok = jnp.min(lowest) >= SAFE_LOW
    high_ok = jnp.max(highest) <= SAFE_HIGH

    @pl.when(jnp.logical_not(low_ok & high_ok))
    def _():
        pl.loop(0, beams)(slow_beam)


def on_device(
    queries,
    new_kv,
    newest_key_value,
    ancestor_block_store,
    parent,
    ancestors,
    ancestor_count,
    keep_list,
    w_reward,
):
    devices = lax.axis_size("beam")
    mp = lax.axis_size("mp")
    own = lax.axis_index("beam").reshape(1)
    beam_dev, _, tokens, kv_width = new_kv.shape
    q_width = queries.shape[2]
    heads = q_width // HEAD_SIZE
    kv_heads = kv_width // HEAD_SIZE
    per_group = heads // kv_heads
    pairs = heads // 2
    pairs_kv = pairs // kv_heads
    keep_dev = keep_list.shape[0] // devices
    blocks = ancestor_block_store.shape[0]
    pack_rows = 3 * tokens + 2 * per_group
    packed = jax.ShapeDtypeStruct((pack_rows, kv_width), new_kv.dtype)
    weight = w_reward.reshape(heads, HEAD_SIZE)
    packed_spec = pl.BlockSpec(packed.shape, lambda i, *_: (0, 0))
    weight_spec = pl.BlockSpec((heads, HEAD_SIZE), lambda i, *_: (0, 0))
    dma = pltpu.SemaphoreType.DMA

    sent = pl.pallas_call(
        functools.partial(pack_kernel, beam_dev=beam_dev, keep_dev=keep_dev),
        out_shape=(packed,) * devices,
        grid_spec=pltpu.PrefetchScalarGridSpec(
            num_scalar_prefetch=3,
            grid=(1,),
            in_specs=[weight_spec, ANY, ANY],
            out_specs=(packed_spec,) * devices,
            scratch_shapes=[
                pltpu.VMEM((devices, tokens, kv_width), jnp.bfloat16),
                dma((devices,)),
                dma((devices, 3)),
            ],
        ),
        name="pack",
    )(own, parent, keep_list, weight, newest_key_value, new_kv)

    arrived = [sent[0]] + [None] * (devices - 1)
    for k in range(devices - 1, 0, -1):
        arrived[k] = lax.ppermute(sent[k], "beam", [(i, i ^ k) for i in range(devices)])

    state_shape = (beam_dev, 2, pairs, LANES_BOTH)
    state_spec = pl.BlockSpec(state_shape, lambda i, *_: (0, 0, 0, 0))
    state = pl.pallas_call(
        functools.partial(
            local_kernel, pairs=pairs, pairs_kv=pairs_kv, slots=ancestors.shape[1]
        ),
        out_shape=jax.ShapeDtypeStruct(state_shape, jnp.float32),
        grid_spec=pltpu.PrefetchScalarGridSpec(
            num_scalar_prefetch=3,
            grid=(1,),
            in_specs=[ANY, ANY, ANY, weight_spec],
            out_specs=state_spec,
            scratch_shapes=[
                pltpu.VMEM(queries.shape, jnp.bfloat16),
                pltpu.VMEM(new_kv.shape, jnp.bfloat16),
                pltpu.VMEM((2, blocks, tokens, kv_width), jnp.bfloat16),
                pltpu.VMEM((pairs, HEAD_SIZE, LANES_BOTH), jnp.bfloat16),
                pltpu.VMEM((blocks, kv_heads, tokens, LANES_BOTH), jnp.bfloat16),
                pltpu.VMEM((pairs, blocks * tokens, LANES_BOTH), jnp.float32),
                dma((beam_dev,)),
                dma((beam_dev,)),
                dma((2,)),
            ],
        ),
        cost_estimate=pl.CostEstimate(
            flops=20_000_000_000, transcendentals=20_000_000, bytes_accessed=16_000_000
        ),
        name="local",
    )(own, ancestors.T, ancestor_count, queries, new_kv, ancestor_block_store, weight)

    partial_reward, kept_blocks = pl.pallas_call(
        functools.partial(
            parent_kernel, devices=devices, pairs=pairs, pairs_kv=pairs_kv
        ),
        out_shape=(
            jax.ShapeDtypeStruct((beam_dev, tokens), jnp.float32),
            jax.ShapeDtypeStruct((keep_dev,) + new_kv.shape[1:], new_kv.dtype),
        ),
        grid_spec=pltpu.PrefetchScalarGridSpec(
            num_scalar_prefetch=5,
            grid=(1,),
            in_specs=[state_spec, weight_spec] + [ANY] * 3 + [packed_spec] * devices,
            out_specs=(
                pl.BlockSpec((beam_dev, tokens), lambda i, *_: (0, 0)),
                ANY,
            ),
            scratch_shapes=[
                pltpu.VMEM(queries.shape, jnp.bfloat16),
                pltpu.VMEM((devices, tokens + 2 * per_group, kv_width), jnp.bfloat16),
                pltpu.VMEM((devices, 2 * tokens, kv_width), jnp.bfloat16),
                pltpu.VMEM((2, tokens, kv_width), jnp.bfloat16),
                pltpu.VMEM((3, pairs, 8, LANES_BOTH), jnp.float32),
                dma((beam_dev,)),
                dma((devices,)),
                dma((devices,)),
                dma((keep_dev, 2)),
                dma(()),
            ],
        ),
        name="parents",
    )(
        own,
        parent,
        keep_list,
        ancestors.T,
        ancestor_count,
        state,
        weight,
        queries,
        new_kv,
        ancestor_block_store,
        *arrived,
    )

    reward = partial_reward
    for shift in range(1, mp):
        ring = [(i, i ^ shift) for i in range(mp)]
        reward = reward + lax.ppermute(partial_reward, "mp", ring)
    return (reward, kept_blocks)


def solution(mesh):
    placed = (
        P("beam", None, "mp"),
        P("beam", None, None, "mp"),
        P("beam", None, None, "mp"),
        P("beam", None, None, "mp"),
        P(),
        P("beam", None),
        P("beam"),
        P(),
        P("mp"),
    )
    return jax.shard_map(
        on_device,
        mesh=mesh,
        in_specs=placed,
        out_specs=(P("beam", None), P("beam", None, None, "mp")),
        check_vma=False,
    )
```

```python
import functools
import math

import jax
import jax.numpy as jnp
from jax import lax
from jax.experimental import pallas as pl
from jax.experimental.pallas import tpu as pltpu
from jax.sharding import PartitionSpec as P

HEAD_SIZE = 128
CHILD = 2
LOG2_SCALE = HEAD_SIZE ** (-0.5) * math.log2(math.e)
MASKED = -1e30
SAFE_LOW = 2.0**-60
SAFE_HIGH = 2.0**100
LANES_BOTH = 2 * HEAD_SIZE
AHEAD = 4
IN_HBM = pl.BlockSpec(memory_space=pltpu.HBM)
IN_VMEM = pl.BlockSpec(memory_space=pltpu.VMEM)
ANY = pl.BlockSpec(memory_space=pl.ANY)


def dot_last(a, b):
    return lax.dot_general(
        a, b, (((1,), (1,)), ((), ())), preferred_element_type=jnp.float32
    )


def dot_first(a, b):
    return lax.dot_general(
        a, b, (((0,), (0,)), ((), ())), preferred_element_type=jnp.float32
    )


def one_hot_rows(rows, period, first):
    shape = (rows, LANES_BOTH)
    row = lax.broadcasted_iota(jnp.int32, shape, 0) % period
    head = first + lax.broadcasted_iota(jnp.int32, shape, 1) // HEAD_SIZE
    return jnp.where(row == head, 1.0, 0.0).astype(jnp.bfloat16)


def lane_rows(rows, period):
    shape = (rows, HEAD_SIZE)
    row = lax.broadcasted_iota(jnp.int32, shape, 0) % period
    lane = lax.broadcasted_iota(jnp.int32, shape, 1)
    return jnp.where(row == lane, 1.0, 0.0).astype(jnp.bfloat16)


def spread_columns(columns, first):
    shape = (columns.shape[0], HEAD_SIZE)
    return jnp.concatenate(
        [
            jnp.broadcast_to(columns[:, first : first + 1], shape),
            jnp.broadcast_to(columns[:, first + 1 : first + 2], shape),
        ],
        axis=1,
    )


def split_keys(keys):
    scaled = keys.astype(jnp.float32) * LOG2_SCALE
    high = scaled.astype(jnp.bfloat16)
    low = (scaled - high.astype(jnp.float32)).astype(jnp.bfloat16)
    return jnp.concatenate([high, low], axis=1)


def kv_lanes(kv):
    return slice(kv * HEAD_SIZE, (kv + 1) * HEAD_SIZE)


def query_pair(query, beam, pair):
    start = pair * LANES_BOTH
    return jnp.concatenate(
        [
            query[beam, :, start : start + HEAD_SIZE],
            query[beam, :, start + HEAD_SIZE : start + LANES_BOTH],
        ],
        axis=0,
    )


def weigh(scores, sums):
    weights = jnp.exp2(scores).reshape(-1, 8, LANES_BOTH)
    return (
        jnp.sum(weights * sums.reshape(weights.shape), axis=0),
        jnp.sum(weights, axis=0),
    )


def row_sum(x):
    return jnp.sum(x, axis=0, keepdims=True)


def causal(tokens):
    shape = (tokens, LANES_BOTH)
    key_pos = lax.broadcasted_iota(jnp.int32, shape, 0)
    token_pos = lax.broadcasted_iota(jnp.int32, shape, 1) % tokens
    return key_pos <= token_pos


def find_row(table, start, step, count, first, beam_dev):
    found = jnp.int32(0)
    for i in range(count):
        row = table[start + i * step] - first
        found = jnp.where((row >= 0) & (row < beam_dev), row, found)
    return found


def pack_kernel(own_ref, parent_ref, keep_ref, weight_ref, newest_ref, new_ref, *rest, beam_dev, keep_dev):
    devices = len(rest) - 3
    outs = rest[:devices]
    value_buf, value_sem, rest_sem = rest[devices:]
    groups = beam_dev // CHILD
    first = own_ref[0] * beam_dev
    tokens = newest_ref.shape[2]
    kv_heads = newest_ref.shape[3] // HEAD_SIZE
    per_group = weight_ref.shape[0] // kv_heads

    def loads(k, row, kept):
        out = outs[k]
        return (
            pltpu.make_async_copy(
                newest_ref.at[row, 1], value_buf.at[k], value_sem.at[k]
            ),
            pltpu.make_async_copy(
                newest_ref.at[row, 0],
                out.at[pl.ds(2 * tokens, tokens)],
                rest_sem.at[k, 0],
            ),
            pltpu.make_async_copy(
                new_ref.at[kept, 0], out.at[pl.ds(0, tokens)], rest_sem.at[k, 1]
            ),
            pltpu.make_async_copy(
                new_ref.at[kept, 1], out.at[pl.ds(tokens, tokens)], rest_sem.at[k, 2]
            ),
        )

    for k in range(devices):
        peer = own_ref[0] ^ k
        row = find_row(parent_ref, peer * beam_dev, CHILD, groups, first, beam_dev)
        kept = find_row(keep_ref, peer * keep_dev, 1, keep_dev, first, beam_dev)
        for copy in loads(k, row, kept):
            copy.start()
    for k in range(devices):
        value_copy = loads(k, 0, 0)[0]
        value_copy.wait()
        for kv in range(kv_heads):
            total = dot_last(
                weight_ref[kv * per_group : (kv + 1) * per_group],
                value_buf[k, :, kv_lanes(kv)],
            )
            high = total.astype(jnp.bfloat16)
            low = (total - high.astype(jnp.float32)).astype(jnp.bfloat16)
            outs[k][3 * tokens : 3 * tokens + per_group, kv_lanes(kv)] = high
            outs[k][3 * tokens + per_group :, kv_lanes(kv)] = low
    for k in range(devices):
        for copy in loads(k, 0, 0)[1:]:
            copy.wait()


def local_kernel(
    own_ref,
    block_ids,
    live_count,
    query_any,
    new_any,
    store_any,
    weight_ref,
    state_ref,
    query_buf,
    new_buf,
    store_buf,
    spread_ref,
    keys_ref,
    sums_ref,
    query_sem,
    new_sem,
    store_sem,
    *,
    pairs,
    pairs_kv,
    slots,
):
    beams, tokens = query_buf.shape[:2]
    blocks = store_buf.shape[1]
    heads = weight_ref.shape[0]
    kv_heads = pairs // pairs_kv
    depth = min(AHEAD, beams)

    def store_copies():
        return [
            pltpu.make_async_copy(
                store_any.at[:, side], store_buf.at[side], store_sem.at[side]
            )
            for side in (1, 0)
        ]

    def beam_copies(b):
        return (
            pltpu.make_async_copy(query_any.at[b], query_buf.at[b], query_sem.at[b]),
            pltpu.make_async_copy(new_any.at[b], new_buf.at[b], new_sem.at[b]),
        )

    for copy in store_copies():
        copy.start()
    for pair in range(pairs):
        spread_ref[pair] = dot_first(
            weight_ref[...], one_hot_rows(heads, heads, 2 * pair)
        ).astype(jnp.bfloat16)
    for copy in store_copies():
        copy.wait()
    for b in range(depth):
        for copy in beam_copies(b):
            copy.start()
    for pair in range(pairs):
        values = store_buf[1, :, :, kv_lanes(pair // pairs_kv)]
        sums_ref[pair] = jnp.dot(
            values.reshape(blocks * tokens, HEAD_SIZE),
            spread_ref[pair],
            preferred_element_type=jnp.float32,
        )

    @pl.loop(0, blocks)
    def _(block):
        for kv in range(kv_heads):
            keys_ref[block, kv] = split_keys(store_buf[0, block, :, kv_lanes(kv)])

    allowed = causal(tokens)
    turned = dot_first(weight_ref[...], lane_rows(heads, heads)).astype(jnp.bfloat16)

    def beam_body(b, count):
        ids = [block_ids[i, b] - own_ref[0] * blocks for i in range(count)]
        for kv in range(kv_heads):
            keys = [keys_ref[i, kv] for i in ids]
            keys = jnp.concatenate(
                keys + [split_keys(new_buf[b, 0, :, kv_lanes(kv)])], axis=0
            )
            columns = jnp.dot(
                new_buf[b, 1, :, kv_lanes(kv)], turned, preferred_element_type=jnp.float32
            )
            for pair in range(kv * pairs_kv, (kv + 1) * pairs_kv):
                own_sums = spread_columns(columns, 2 * pair)
                query = query_pair(query_buf, b, pair)
                scores = dot_last(keys, jnp.concatenate([query, query], axis=1))
                own_scores = jnp.where(allowed, scores[count * tokens :], MASKED)
                top, bottom = weigh(own_scores, own_sums)
                for i, block in enumerate(ids):
                    sums = sums_ref[pair, pl.ds(pl.multiple_of(block * tokens, tokens), tokens)]
                    more = weigh(scores[i * tokens : (i + 1) * tokens], sums)
                    top, bottom = top + more[0], bottom + more[1]
                state_ref[b, 0, pair : pair + 1] = row_sum(top)
                state_ref[b, 1, pair : pair + 1] = row_sum(bottom)

    @pl.loop(0, beams)
    def _(b):
        @pl.when(b + depth < beams)
        def _():
            for copy in beam_copies(b + depth):
                copy.start()

        for copy in beam_copies(b):
            copy.wait()
        for count in range(1, slots + 1):

            @pl.when(live_count[b] == count)
            def _():
                beam_body(b, count)


def parent_kernel(own_ref, parent_ref, keep_ref, block_ids, live_count, *rest, devices, pairs, pairs_kv):
    state_ref, weight_ref, query_buf, new_any, store_any = rest[:5]
    arrived = rest[5 : 5 + devices]
    reward_ref, kept_ref = rest[5 + devices : 7 + devices]
    (
        parent_buf,
        kept_buf,
        slow_block,
        slow_state,
        parent_sem,
        load_sem,
        store_sem,
        slow_sem,
    ) = rest[7 + devices :]
    beams, tokens = query_buf.shape[:2]
    own = own_ref[0]
    keep_dev = kept_ref.shape[0]
    kv_heads = pairs // pairs_kv
    blocks = store_any.shape[0]
    sum_rows = parent_buf.shape[1] - tokens
    heads = 2 * pairs

    def parent_load(k):
        return pltpu.make_async_copy(
            arrived[k].at[pl.ds(2 * tokens, tokens + sum_rows)],
            parent_buf.at[k],
            parent_sem.at[k],
        )

    def kept_load(k):
        return pltpu.make_async_copy(
            arrived[k].at[pl.ds(0, 2 * tokens)], kept_buf.at[k], load_sem.at[k]
        )

    def kept_stores(j, k):
        return [
            pltpu.make_async_copy(
                kept_buf.at[k, pl.ds(side * tokens, tokens)],
                kept_ref.at[j, side],
                store_sem.at[j, side],
            )
            for side in range(2)
        ]

    def slot_of(b):
        return (parent_ref[own * beams + b] // beams) ^ own

    for k in range(devices):
        parent_load(k).start()
    for k in range(devices):
        kept_load(k).start()
    for k in range(devices):
        parent_load(k).wait()

    def group_step(group, limits):
        slot = slot_of(group * CHILD)
        lowest, highest = limits
        totals = [jnp.zeros((1, tokens), jnp.float32) for _ in range(CHILD)]
        for kv in range(kv_heads):
            keys = parent_buf[slot, :tokens, kv_lanes(kv)]
            columns = dot_first(
                parent_buf[slot, tokens:, kv_lanes(kv)],
                lane_rows(sum_rows, sum_rows // 2),
            )
            for pair in range(kv * pairs_kv, (kv + 1) * pairs_kv):
                sums = spread_columns(columns, 2 * (pair % pairs_kv))
                for child in range(CHILD):
                    b = group * CHILD + child
                    query = query_pair(query_buf, b, pair)
                    scores = dot_last(keys, query) * LOG2_SCALE
                    top, bottom = weigh(scores, sums)
                    top = row_sum(top) + state_ref[b, 0, pair : pair + 1]
                    bottom = row_sum(bottom) + state_ref[b, 1, pair : pair + 1]
                    lowest = jnp.minimum(lowest, bottom)
                    highest = jnp.maximum(highest, bottom)
                    ratio = top / bottom
                    totals[child] += ratio[:, :tokens] + ratio[:, tokens:]
        for child in range(CHILD):
            reward_ref[pl.ds(group * CHILD + child, 1), :] = totals[child]
        return lowest, highest

    def start_kept():
        for k in range(devices):
            kept_load(k).wait()

        @pl.loop(0, keep_dev)
        def _(j):
            k = (keep_ref[own * keep_dev + j] // beams) ^ own
            for copy in kept_stores(j, k):
                copy.start()

    limits = (
        jnp.full((1, LANES_BOTH), SAFE_HIGH, jnp.float32),
        jnp.full((1, LANES_BOTH), SAFE_LOW, jnp.float32),
    )
    groups = beams // CHILD
    limits = lax.fori_loop(0, groups // 2, group_step, limits)
    start_kept()
    lowest, highest = lax.fori_loop(groups // 2, groups, group_step, limits)

    @pl.loop(0, keep_dev)
    def _(j):
        for copy in kept_stores(j, 0):
            copy.wait()

    def fetch(source, target):
        copy = pltpu.make_async_copy(source, target, slow_sem)
        copy.start()
        copy.wait()

    def online_step(b, pair, keys, sums, allowed=None):
        start = pl.multiple_of(pair * LANES_BOTH, LANES_BOTH)
        query = jnp.concatenate(
            [
                query_buf[b, :, pl.ds(start, HEAD_SIZE)],
                query_buf[b, :, pl.ds(start + HEAD_SIZE, HEAD_SIZE)],
            ],
            axis=0,
        )
        scores = dot_last(keys, query)
        if allowed is not None:
            scores = jnp.where(allowed, scores, MASKED)
        scores = scores.reshape(-1, 8, LANES_BOTH)
        before = slow_state[0, pair]
        after = jnp.maximum(before, jnp.max(scores, axis=0))
        fade = jnp.exp2((before - after) * LOG2_SCALE)
        weights = jnp.exp2((scores - after[None]) * LOG2_SCALE)
        sums = sums.reshape(weights.shape)
        slow_state[0, pair] = after
        slow_state[1, pair] = slow_state[1, pair] * fade + jnp.sum(weights * sums, axis=0)
        slow_state[2, pair] = slow_state[2, pair] * fade + jnp.sum(weights, axis=0)

    def slow_lanes(pair):
        return pl.ds(pl.multiple_of(pair // pairs_kv * HEAD_SIZE, HEAD_SIZE), HEAD_SIZE)

    def slow_plain(b, pair, allowed=None):
        spread = dot_first(weight_ref[...], one_hot_rows(heads, heads, 2 * pair))
        sums = jnp.dot(
            slow_block[1, :, slow_lanes(pair)],
            spread.astype(jnp.bfloat16),
            preferred_element_type=jnp.float32,
        )
        online_step(b, pair, slow_block[0, :, slow_lanes(pair)], sums, allowed)

    def slow_beam(b):
        slow_state[0] = jnp.full(slow_state.shape[1:], MASKED, jnp.float32)
        slow_state[1] = jnp.zeros(slow_state.shape[1:], jnp.float32)
        slow_state[2] = jnp.zeros(slow_state.shape[1:], jnp.float32)

        @pl.loop(0, live_count[b])
        def _(i):
            fetch(store_any.at[block_ids[i, b] - own * blocks], slow_block)
            pl.loop(0, pairs)(lambda pair: slow_plain(b, pair))

        fetch(new_any.at[b], slow_block)
        pl.loop(0, pairs)(lambda pair: slow_plain(b, pair, causal(tokens)))
        here = slot_of(b)
        reward_ref[pl.ds(b, 1), :] = jnp.zeros((1, tokens), jnp.float32)

        @pl.loop(0, pairs)
        def _(pair):
            sums = dot_first(
                parent_buf[here, tokens:, slow_lanes(pair)],
                one_hot_rows(sum_rows, sum_rows // 2, 2 * (pair % pairs_kv)),
            )
            online_step(b, pair, parent_buf[here, :tokens, slow_lanes(pair)], sums)
            state = slow_state[0, pair]
            row_max = jnp.max(state, axis=0, keepdims=True)
            fade = jnp.exp2((state - row_max) * LOG2_SCALE)
            ratio = jnp.sum(slow_state[1, pair] * fade, axis=0, keepdims=True) / jnp.sum(
                slow_state[2, pair] * fade, axis=0, keepdims=True
            )
            reward_ref[pl.ds(b, 1), :] += ratio[:, :tokens] + ratio[:, tokens:]

    low_ok = jnp.min(lowest) >= SAFE_LOW
    high_ok = jnp.max(highest) <= SAFE_HIGH

    @pl.when(jnp.logical_not(low_ok & high_ok))
    def _():
        pl.loop(0, beams)(slow_beam)


def on_device(
    queries,
    new_kv,
    newest_key_value,
    ancestor_block_store,
    parent,
    ancestors,
    ancestor_count,
    keep_list,
    w_reward,
):
    devices = lax.axis_size("beam")
    mp = lax.axis_size("mp")
    own = lax.axis_index("beam").reshape(1)
    beam_dev, _, tokens, kv_width = new_kv.shape
    q_width = queries.shape[2]
    heads = q_width // HEAD_SIZE
    kv_heads = kv_width // HEAD_SIZE
    per_group = heads // kv_heads
    pairs = heads // 2
    pairs_kv = pairs // kv_heads
    keep_dev = keep_list.shape[0] // devices
    blocks = ancestor_block_store.shape[0]
    pack_rows = 3 * tokens + 2 * per_group
    packed = jax.ShapeDtypeStruct((pack_rows, kv_width), new_kv.dtype)
    weight = w_reward.reshape(heads, HEAD_SIZE)
    weight_spec = pl.BlockSpec((heads, HEAD_SIZE), lambda i, *_: (0, 0))
    dma = pltpu.SemaphoreType.DMA

    sent = pl.pallas_call(
        functools.partial(pack_kernel, beam_dev=beam_dev, keep_dev=keep_dev),
        out_shape=(pltpu.VMEM(packed.shape, packed.dtype),) * devices,
        grid_spec=pltpu.PrefetchScalarGridSpec(
            num_scalar_prefetch=3,
            grid=(1,),
            in_specs=[weight_spec, IN_HBM, IN_HBM],
            out_specs=(IN_VMEM,) * devices,
            scratch_shapes=[
                pltpu.VMEM((devices, tokens, kv_width), jnp.bfloat16),
                dma((devices,)),
                dma((devices, 3)),
            ],
        ),
        compiler_params=pltpu.CompilerParams(vmem_limit_bytes=16 << 20),
        name="pack",
    )(
        own,
        parent,
        keep_list,
        weight,
        pltpu.with_memory_space_constraint(newest_key_value, pltpu.HBM),
        pltpu.with_memory_space_constraint(new_kv, pltpu.HBM),
    )

    arrived = [sent[0]] + [None] * (devices - 1)
    for k in range(devices - 1, 0, -1):
        arrived[k] = lax.ppermute(sent[k], "beam", [(i, i ^ k) for i in range(devices)])

    state_shape = (beam_dev, 2, pairs, LANES_BOTH)
    state, near_queries = pl.pallas_call(
        functools.partial(
            local_kernel, pairs=pairs, pairs_kv=pairs_kv, slots=ancestors.shape[1]
        ),
        out_shape=(
            pltpu.VMEM(state_shape, jnp.float32),
            pltpu.VMEM(queries.shape, queries.dtype),
        ),
        grid_spec=pltpu.PrefetchScalarGridSpec(
            num_scalar_prefetch=3,
            grid=(1,),
            in_specs=[ANY, ANY, ANY, weight_spec],
            out_specs=(IN_VMEM, IN_VMEM),
            scratch_shapes=[
                pltpu.VMEM(new_kv.shape, jnp.bfloat16),
                pltpu.VMEM((2, blocks, tokens, kv_width), jnp.bfloat16),
                pltpu.VMEM((pairs, HEAD_SIZE, LANES_BOTH), jnp.bfloat16),
                pltpu.VMEM((blocks, kv_heads, tokens, LANES_BOTH), jnp.bfloat16),
                pltpu.VMEM((pairs, blocks * tokens, LANES_BOTH), jnp.float32),
                dma((beam_dev,)),
                dma((beam_dev,)),
                dma((2,)),
            ],
        ),
        cost_estimate=pl.CostEstimate(
            flops=20_000_000_000, transcendentals=20_000_000, bytes_accessed=16_000_000
        ),
        compiler_params=pltpu.CompilerParams(vmem_limit_bytes=28 << 20),
        name="local",
    )(own, ancestors.T, ancestor_count, queries, new_kv, ancestor_block_store, weight)

    partial_reward, kept_blocks = pl.pallas_call(
        functools.partial(
            parent_kernel, devices=devices, pairs=pairs, pairs_kv=pairs_kv
        ),
        out_shape=(
            jax.ShapeDtypeStruct((beam_dev, tokens), jnp.float32),
            jax.ShapeDtypeStruct((keep_dev,) + new_kv.shape[1:], new_kv.dtype),
        ),
        grid_spec=pltpu.PrefetchScalarGridSpec(
            num_scalar_prefetch=5,
            grid=(1,),
            in_specs=[IN_VMEM, weight_spec, IN_VMEM, ANY, ANY] + [IN_VMEM] * devices,
            out_specs=(
                pl.BlockSpec((beam_dev, tokens), lambda i, *_: (0, 0)),
                ANY,
            ),
            scratch_shapes=[
                pltpu.VMEM((devices, tokens + 2 * per_group, kv_width), jnp.bfloat16),
                pltpu.VMEM((devices, 2 * tokens, kv_width), jnp.bfloat16),
                pltpu.VMEM((2, tokens, kv_width), jnp.bfloat16),
                pltpu.VMEM((3, pairs, 8, LANES_BOTH), jnp.float32),
                dma((devices,)),
                dma((devices,)),
                dma((keep_dev, 2)),
                dma(()),
            ],
        ),
        compiler_params=pltpu.CompilerParams(vmem_limit_bytes=16 << 20),
        name="parents",
    )(
        own,
        parent,
        keep_list,
        ancestors.T,
        ancestor_count,
        pltpu.with_memory_space_constraint(state, pltpu.VMEM),
        weight,
        pltpu.with_memory_space_constraint(near_queries, pltpu.VMEM),
        new_kv,
        ancestor_block_store,
        *[pltpu.with_memory_space_constraint(x, pltpu.VMEM) for x in arrived],
    )

    reward = partial_reward
    for shift in range(1, mp):
        ring = [(i, i ^ shift) for i in range(mp)]
        reward = reward + lax.ppermute(partial_reward, "mp", ring)
    return (reward, kept_blocks)


def solution(mesh):
    placed = (
        P("beam", None, "mp"),
        P("beam", None, None, "mp"),
        P("beam", None, None, "mp"),
        P("beam", None, None, "mp"),
        P(),
        P("beam", None),
        P("beam"),
        P(),
        P("mp"),
    )
    return jax.shard_map(
        on_device,
        mesh=mesh,
        in_specs=placed,
        out_specs=(P("beam", None), P("beam", None, None, "mp")),
        check_vma=False,
    )
```

```python
import functools
import math

import jax
import jax.numpy as jnp
from jax import lax
from jax.experimental import pallas as pl
from jax.experimental.pallas import tpu as pltpu
from jax.sharding import PartitionSpec as P

HEAD_SIZE = 128
CHILD = 2
LOG2_SCALE = HEAD_SIZE ** (-0.5) * math.log2(math.e)
MASKED = -1e30
SAFE_LOW = 2.0**-60
SAFE_HIGH = 2.0**100
LANES_BOTH = 2 * HEAD_SIZE
AHEAD = 4
IN_HBM = pl.BlockSpec(memory_space=pltpu.HBM)
IN_VMEM = pl.BlockSpec(memory_space=pltpu.VMEM)
ANY = pl.BlockSpec(memory_space=pl.ANY)


def dot_last(a, b):
    return lax.dot_general(
        a, b, (((1,), (1,)), ((), ())), preferred_element_type=jnp.float32
    )


def dot_first(a, b):
    return lax.dot_general(
        a, b, (((0,), (0,)), ((), ())), preferred_element_type=jnp.float32
    )


def one_hot_rows(rows, period, first):
    shape = (rows, LANES_BOTH)
    row = lax.broadcasted_iota(jnp.int32, shape, 0) % period
    head = first + lax.broadcasted_iota(jnp.int32, shape, 1) // HEAD_SIZE
    return jnp.where(row == head, 1.0, 0.0).astype(jnp.bfloat16)


def lane_rows(rows, period):
    shape = (rows, HEAD_SIZE)
    row = lax.broadcasted_iota(jnp.int32, shape, 0) % period
    lane = lax.broadcasted_iota(jnp.int32, shape, 1)
    return jnp.where(row == lane, 1.0, 0.0).astype(jnp.bfloat16)


def spread_columns(columns, first):
    shape = (columns.shape[0], HEAD_SIZE)
    return jnp.concatenate(
        [
            jnp.broadcast_to(columns[:, first : first + 1], shape),
            jnp.broadcast_to(columns[:, first + 1 : first + 2], shape),
        ],
        axis=1,
    )


def split_keys(keys):
    scaled = keys.astype(jnp.float32) * LOG2_SCALE
    high = scaled.astype(jnp.bfloat16)
    low = (scaled - high.astype(jnp.float32)).astype(jnp.bfloat16)
    return jnp.concatenate([high, low], axis=1)


def kv_lanes(kv):
    return slice(kv * HEAD_SIZE, (kv + 1) * HEAD_SIZE)


def query_pair(query, beam, pair):
    start = pair * LANES_BOTH
    return jnp.concatenate(
        [
            query[beam, :, start : start + HEAD_SIZE],
            query[beam, :, start + HEAD_SIZE : start + LANES_BOTH],
        ],
        axis=0,
    )


def weigh(scores, sums):
    weights = jnp.exp2(scores).reshape(-1, 8, LANES_BOTH)
    return (
        jnp.sum(weights * sums.reshape(weights.shape), axis=0),
        jnp.sum(weights, axis=0),
    )


def row_sum(x):
    return jnp.sum(x, axis=0, keepdims=True)


def causal(tokens):
    shape = (tokens, LANES_BOTH)
    key_pos = lax.broadcasted_iota(jnp.int32, shape, 0)
    token_pos = lax.broadcasted_iota(jnp.int32, shape, 1) % tokens
    return key_pos <= token_pos


def find_row(table, start, step, count, first, beam_dev):
    found = jnp.int32(0)
    for i in range(count):
        row = table[start + i * step] - first
        found = jnp.where((row >= 0) & (row < beam_dev), row, found)
    return found


def pack_kernel(own_ref, parent_ref, keep_ref, weight_ref, newest_ref, new_ref, *rest, beam_dev, keep_dev):
    devices = len(rest) - 3
    outs = rest[:devices]
    value_buf, value_sem, rest_sem = rest[devices:]
    groups = beam_dev // CHILD
    first = own_ref[0] * beam_dev
    tokens = newest_ref.shape[2]
    kv_heads = newest_ref.shape[3] // HEAD_SIZE
    per_group = weight_ref.shape[0] // kv_heads

    def loads(k, row, kept):
        out = outs[k]
        return (
            pltpu.make_async_copy(
                newest_ref.at[row, 1], value_buf.at[k], value_sem.at[k]
            ),
            pltpu.make_async_copy(
                newest_ref.at[row, 0],
                out.at[pl.ds(2 * tokens, tokens)],
                rest_sem.at[k, 0],
            ),
            pltpu.make_async_copy(
                new_ref.at[kept, 0], out.at[pl.ds(0, tokens)], rest_sem.at[k, 1]
            ),
            pltpu.make_async_copy(
                new_ref.at[kept, 1], out.at[pl.ds(tokens, tokens)], rest_sem.at[k, 2]
            ),
        )

    for k in range(devices):
        peer = own_ref[0] ^ k
        row = find_row(parent_ref, peer * beam_dev, CHILD, groups, first, beam_dev)
        kept = find_row(keep_ref, peer * keep_dev, 1, keep_dev, first, beam_dev)
        for copy in loads(k, row, kept):
            copy.start()
    for k in range(devices):
        value_copy = loads(k, 0, 0)[0]
        value_copy.wait()
        for kv in range(kv_heads):
            total = dot_last(
                weight_ref[kv * per_group : (kv + 1) * per_group],
                value_buf[k, :, kv_lanes(kv)],
            )
            high = total.astype(jnp.bfloat16)
            low = (total - high.astype(jnp.float32)).astype(jnp.bfloat16)
            outs[k][3 * tokens : 3 * tokens + per_group, kv_lanes(kv)] = high
            outs[k][3 * tokens + per_group :, kv_lanes(kv)] = low
    for k in range(devices):
        for copy in loads(k, 0, 0)[1:]:
            copy.wait()


def local_kernel(
    own_ref,
    block_ids,
    live_count,
    query_any,
    new_any,
    store_any,
    weight_ref,
    state_ref,
    query_buf,
    new_buf,
    store_buf,
    spread_ref,
    keys_ref,
    sums_ref,
    query_sem,
    new_sem,
    store_sem,
    *,
    pairs,
    pairs_kv,
    slots,
):
    beams, tokens = query_buf.shape[:2]
    blocks = store_buf.shape[1]
    heads = weight_ref.shape[0]
    kv_heads = pairs // pairs_kv
    depth = min(AHEAD, beams)

    def store_copies():
        return [
            pltpu.make_async_copy(
                store_any.at[:, side], store_buf.at[side], store_sem.at[side]
            )
            for side in (1, 0)
        ]

    def beam_copies(b):
        return (
            pltpu.make_async_copy(query_any.at[b], query_buf.at[b], query_sem.at[b]),
            pltpu.make_async_copy(new_any.at[b], new_buf.at[b], new_sem.at[b]),
        )

    for copy in store_copies():
        copy.start()
    for pair in range(pairs):
        spread_ref[pair] = dot_first(
            weight_ref[...], one_hot_rows(heads, heads, 2 * pair)
        ).astype(jnp.bfloat16)
    for copy in store_copies():
        copy.wait()
    for b in range(depth):
        for copy in beam_copies(b):
            copy.start()
    for pair in range(pairs):
        values = store_buf[1, :, :, kv_lanes(pair // pairs_kv)]
        sums_ref[pair] = jnp.dot(
            values.reshape(blocks * tokens, HEAD_SIZE),
            spread_ref[pair],
            preferred_element_type=jnp.float32,
        )

    @pl.loop(0, blocks)
    def _(block):
        for kv in range(kv_heads):
            keys_ref[block, kv] = split_keys(store_buf[0, block, :, kv_lanes(kv)])

    allowed = causal(tokens)
    turned = dot_first(weight_ref[...], lane_rows(heads, heads)).astype(jnp.bfloat16)

    def beam_body(b, count):
        ids = [block_ids[i, b] - own_ref[0] * blocks for i in range(count)]
        for kv in range(kv_heads):
            keys = [keys_ref[i, kv] for i in ids]
            keys = jnp.concatenate(
                keys + [split_keys(new_buf[b, 0, :, kv_lanes(kv)])], axis=0
            )
            columns = jnp.dot(
                new_buf[b, 1, :, kv_lanes(kv)], turned, preferred_element_type=jnp.float32
            )
            for pair in range(kv * pairs_kv, (kv + 1) * pairs_kv):
                own_sums = spread_columns(columns, 2 * pair)
                query = query_pair(query_buf, b, pair)
                scores = dot_last(keys, jnp.concatenate([query, query], axis=1))
                own_scores = jnp.where(allowed, scores[count * tokens :], MASKED)
                top, bottom = weigh(own_scores, own_sums)
                for i, block in enumerate(ids):
                    sums = sums_ref[pair, pl.ds(pl.multiple_of(block * tokens, tokens), tokens)]
                    more = weigh(scores[i * tokens : (i + 1) * tokens], sums)
                    top, bottom = top + more[0], bottom + more[1]
                state_ref[b, 0, pair : pair + 1] = row_sum(top)
                state_ref[b, 1, pair : pair + 1] = row_sum(bottom)

    @pl.loop(0, beams)
    def _(b):
        @pl.when(b + depth < beams)
        def _():
            for copy in beam_copies(b + depth):
                copy.start()

        for copy in beam_copies(b):
            copy.wait()
        for count in range(1, slots + 1):

            @pl.when(live_count[b] == count)
            def _():
                beam_body(b, count)


def parent_kernel(own_ref, parent_ref, keep_ref, block_ids, live_count, *rest, devices, pairs, pairs_kv):
    state_ref, weight_ref, query_buf, new_any, store_any = rest[:5]
    arrived = rest[5 : 5 + devices]
    reward_ref, kept_ref = rest[5 + devices : 7 + devices]
    (
        parent_buf,
        kept_buf,
        slow_block,
        slow_state,
        parent_sem,
        load_sem,
        store_sem,
        slow_sem,
    ) = rest[7 + devices :]
    beams, tokens = query_buf.shape[:2]
    own = own_ref[0]
    keep_dev = kept_ref.shape[0]
    kv_heads = pairs // pairs_kv
    blocks = store_any.shape[0]
    sum_rows = parent_buf.shape[1] - tokens
    heads = 2 * pairs

    def parent_load(k):
        return pltpu.make_async_copy(
            arrived[k].at[pl.ds(2 * tokens, tokens + sum_rows)],
            parent_buf.at[k],
            parent_sem.at[k],
        )

    def kept_load(k):
        return pltpu.make_async_copy(
            arrived[k].at[pl.ds(0, 2 * tokens)], kept_buf.at[k], load_sem.at[k]
        )

    def kept_stores(j, k):
        return [
            pltpu.make_async_copy(
                kept_buf.at[k, pl.ds(side * tokens, tokens)],
                kept_ref.at[j, side],
                store_sem.at[j, side],
            )
            for side in range(2)
        ]

    def slot_of(b):
        return (parent_ref[own * beams + b] // beams) ^ own

    for k in range(devices):
        parent_load(k).start()
    for k in range(devices):
        kept_load(k).start()
    for k in range(devices):
        parent_load(k).wait()

    def group_step(group, limits):
        slot = slot_of(group * CHILD)
        lowest, highest = limits
        totals = [jnp.zeros((1, tokens), jnp.float32) for _ in range(CHILD)]
        for kv in range(kv_heads):
            keys = parent_buf[slot, :tokens, kv_lanes(kv)]
            columns = dot_first(
                parent_buf[slot, tokens:, kv_lanes(kv)],
                lane_rows(sum_rows, sum_rows // 2),
            )
            for pair in range(kv * pairs_kv, (kv + 1) * pairs_kv):
                sums = spread_columns(columns, 2 * (pair % pairs_kv))
                for child in range(CHILD):
                    b = group * CHILD + child
                    query = query_pair(query_buf, b, pair)
                    scores = dot_last(keys, query) * LOG2_SCALE
                    top, bottom = weigh(scores, sums)
                    top = row_sum(top) + state_ref[b, 0, pair : pair + 1]
                    bottom = row_sum(bottom) + state_ref[b, 1, pair : pair + 1]
                    lowest = jnp.minimum(lowest, bottom)
                    highest = jnp.maximum(highest, bottom)
                    ratio = top / bottom
                    totals[child] += ratio[:, :tokens] + ratio[:, tokens:]
        for child in range(CHILD):
            reward_ref[pl.ds(group * CHILD + child, 1), :] = totals[child]
        return lowest, highest

    def start_kept():
        for k in range(devices):
            kept_load(k).wait()

        @pl.loop(0, keep_dev)
        def _(j):
            k = (keep_ref[own * keep_dev + j] // beams) ^ own
            for copy in kept_stores(j, k):
                copy.start()

    limits = (
        jnp.full((1, LANES_BOTH), SAFE_HIGH, jnp.float32),
        jnp.full((1, LANES_BOTH), SAFE_LOW, jnp.float32),
    )
    groups = beams // CHILD
    limits = lax.fori_loop(0, groups // 2, group_step, limits)
    start_kept()
    lowest, highest = lax.fori_loop(groups // 2, groups, group_step, limits)

    @pl.loop(0, keep_dev)
    def _(j):
        for copy in kept_stores(j, 0):
            copy.wait()

    def fetch(source, target):
        copy = pltpu.make_async_copy(source, target, slow_sem)
        copy.start()
        copy.wait()

    def online_step(b, pair, keys, sums, allowed=None):
        start = pl.multiple_of(pair * LANES_BOTH, LANES_BOTH)
        query = jnp.concatenate(
            [
                query_buf[b, :, pl.ds(start, HEAD_SIZE)],
                query_buf[b, :, pl.ds(start + HEAD_SIZE, HEAD_SIZE)],
            ],
            axis=0,
        )
        scores = dot_last(keys, query)
        if allowed is not None:
            scores = jnp.where(allowed, scores, MASKED)
        scores = scores.reshape(-1, 8, LANES_BOTH)
        before = slow_state[0, pair]
        after = jnp.maximum(before, jnp.max(scores, axis=0))
        fade = jnp.exp2((before - after) * LOG2_SCALE)
        weights = jnp.exp2((scores - after[None]) * LOG2_SCALE)
        sums = sums.reshape(weights.shape)
        slow_state[0, pair] = after
        slow_state[1, pair] = slow_state[1, pair] * fade + jnp.sum(weights * sums, axis=0)
        slow_state[2, pair] = slow_state[2, pair] * fade + jnp.sum(weights, axis=0)

    def slow_lanes(pair):
        return pl.ds(pl.multiple_of(pair // pairs_kv * HEAD_SIZE, HEAD_SIZE), HEAD_SIZE)

    def slow_plain(b, pair, allowed=None):
        spread = dot_first(weight_ref[...], one_hot_rows(heads, heads, 2 * pair))
        sums = jnp.dot(
            slow_block[1, :, slow_lanes(pair)],
            spread.astype(jnp.bfloat16),
            preferred_element_type=jnp.float32,
        )
        online_step(b, pair, slow_block[0, :, slow_lanes(pair)], sums, allowed)

    def slow_beam(b):
        slow_state[0] = jnp.full(slow_state.shape[1:], MASKED, jnp.float32)
        slow_state[1] = jnp.zeros(slow_state.shape[1:], jnp.float32)
        slow_state[2] = jnp.zeros(slow_state.shape[1:], jnp.float32)

        @pl.loop(0, live_count[b])
        def _(i):
            fetch(store_any.at[block_ids[i, b] - own * blocks], slow_block)
            pl.loop(0, pairs)(lambda pair: slow_plain(b, pair))

        fetch(new_any.at[b], slow_block)
        pl.loop(0, pairs)(lambda pair: slow_plain(b, pair, causal(tokens)))
        here = slot_of(b)
        reward_ref[pl.ds(b, 1), :] = jnp.zeros((1, tokens), jnp.float32)

        @pl.loop(0, pairs)
        def _(pair):
            sums = dot_first(
                parent_buf[here, tokens:, slow_lanes(pair)],
                one_hot_rows(sum_rows, sum_rows // 2, 2 * (pair % pairs_kv)),
            )
            online_step(b, pair, parent_buf[here, :tokens, slow_lanes(pair)], sums)
            state = slow_state[0, pair]
            row_max = jnp.max(state, axis=0, keepdims=True)
            fade = jnp.exp2((state - row_max) * LOG2_SCALE)
            ratio = jnp.sum(slow_state[1, pair] * fade, axis=0, keepdims=True) / jnp.sum(
                slow_state[2, pair] * fade, axis=0, keepdims=True
            )
            reward_ref[pl.ds(b, 1), :] += ratio[:, :tokens] + ratio[:, tokens:]

    low_ok = jnp.min(lowest) >= SAFE_LOW
    high_ok = jnp.max(highest) <= SAFE_HIGH

    @pl.when(jnp.logical_not(low_ok & high_ok))
    def _():
        pl.loop(0, beams)(slow_beam)


def on_device(
    queries,
    new_kv,
    newest_key_value,
    ancestor_block_store,
    parent,
    ancestors,
    ancestor_count,
    keep_list,
    w_reward,
):
    devices = lax.axis_size("beam")
    mp = lax.axis_size("mp")
    own = lax.axis_index("beam").reshape(1)
    beam_dev, _, tokens, kv_width = new_kv.shape
    q_width = queries.shape[2]
    heads = q_width // HEAD_SIZE
    kv_heads = kv_width // HEAD_SIZE
    per_group = heads // kv_heads
    pairs = heads // 2
    pairs_kv = pairs // kv_heads
    keep_dev = keep_list.shape[0] // devices
    blocks = ancestor_block_store.shape[0]
    pack_rows = 3 * tokens + 2 * per_group
    packed = jax.ShapeDtypeStruct((pack_rows, kv_width), new_kv.dtype)
    weight = w_reward.reshape(heads, HEAD_SIZE)
    weight_spec = pl.BlockSpec((heads, HEAD_SIZE), lambda i, *_: (0, 0))
    dma = pltpu.SemaphoreType.DMA

    sent = pl.pallas_call(
        functools.partial(pack_kernel, beam_dev=beam_dev, keep_dev=keep_dev),
        out_shape=(pltpu.VMEM(packed.shape, packed.dtype),) * devices,
        grid_spec=pltpu.PrefetchScalarGridSpec(
            num_scalar_prefetch=3,
            grid=(1,),
            in_specs=[weight_spec, IN_HBM, IN_HBM],
            out_specs=(IN_VMEM,) * devices,
            scratch_shapes=[
                pltpu.VMEM((devices, tokens, kv_width), jnp.bfloat16),
                dma((devices,)),
                dma((devices, 3)),
            ],
        ),
        name="pack",
    )(
        own,
        parent,
        keep_list,
        weight,
        pltpu.with_memory_space_constraint(newest_key_value, pltpu.HBM),
        pltpu.with_memory_space_constraint(new_kv, pltpu.HBM),
    )

    arrived = [sent[0]] + [None] * (devices - 1)
    for k in range(devices - 1, 0, -1):
        arrived[k] = lax.ppermute(sent[k], "beam", [(i, i ^ k) for i in range(devices)])

    state_shape = (beam_dev, 2, pairs, LANES_BOTH)
    state, near_queries = pl.pallas_call(
        functools.partial(
            local_kernel, pairs=pairs, pairs_kv=pairs_kv, slots=ancestors.shape[1]
        ),
        out_shape=(
            pltpu.VMEM(state_shape, jnp.float32),
            pltpu.VMEM(queries.shape, queries.dtype),
        ),
        grid_spec=pltpu.PrefetchScalarGridSpec(
            num_scalar_prefetch=3,
            grid=(1,),
            in_specs=[IN_HBM, ANY, ANY, weight_spec],
            out_specs=(IN_VMEM, IN_VMEM),
            scratch_shapes=[
                pltpu.VMEM(new_kv.shape, jnp.bfloat16),
                pltpu.VMEM((2, blocks, tokens, kv_width), jnp.bfloat16),
                pltpu.VMEM((pairs, HEAD_SIZE, LANES_BOTH), jnp.bfloat16),
                pltpu.VMEM((blocks, kv_heads, tokens, LANES_BOTH), jnp.bfloat16),
                pltpu.VMEM((pairs, blocks * tokens, LANES_BOTH), jnp.float32),
                dma((beam_dev,)),
                dma((beam_dev,)),
                dma((2,)),
            ],
        ),
        cost_estimate=pl.CostEstimate(
            flops=20_000_000_000, transcendentals=20_000_000, bytes_accessed=16_000_000
        ),
        compiler_params=pltpu.CompilerParams(vmem_limit_bytes=28 << 20),
        name="local",
    )(
        own,
        ancestors.T,
        ancestor_count,
        pltpu.with_memory_space_constraint(queries, pltpu.HBM),
        new_kv,
        ancestor_block_store,
        weight,
    )

    partial_reward, kept_blocks = pl.pallas_call(
        functools.partial(
            parent_kernel, devices=devices, pairs=pairs, pairs_kv=pairs_kv
        ),
        out_shape=(
            jax.ShapeDtypeStruct((beam_dev, tokens), jnp.float32),
            jax.ShapeDtypeStruct((keep_dev,) + new_kv.shape[1:], new_kv.dtype),
        ),
        grid_spec=pltpu.PrefetchScalarGridSpec(
            num_scalar_prefetch=5,
            grid=(1,),
            in_specs=[IN_VMEM, weight_spec, IN_VMEM, ANY, ANY] + [IN_VMEM] * devices,
            out_specs=(
                pl.BlockSpec((beam_dev, tokens), lambda i, *_: (0, 0)),
                ANY,
            ),
            scratch_shapes=[
                pltpu.VMEM((devices, tokens + 2 * per_group, kv_width), jnp.bfloat16),
                pltpu.VMEM((devices, 2 * tokens, kv_width), jnp.bfloat16),
                pltpu.VMEM((2, tokens, kv_width), jnp.bfloat16),
                pltpu.VMEM((3, pairs, 8, LANES_BOTH), jnp.float32),
                dma((devices,)),
                dma((devices,)),
                dma((keep_dev, 2)),
                dma(()),
            ],
        ),
        compiler_params=pltpu.CompilerParams(vmem_limit_bytes=16 << 20),
        name="parents",
    )(
        own,
        parent,
        keep_list,
        ancestors.T,
        ancestor_count,
        pltpu.with_memory_space_constraint(state, pltpu.VMEM),
        weight,
        pltpu.with_memory_space_constraint(near_queries, pltpu.VMEM),
        new_kv,
        ancestor_block_store,
        *[pltpu.with_memory_space_constraint(x, pltpu.VMEM) for x in arrived],
    )

    reward = partial_reward
    for shift in range(1, mp):
        ring = [(i, i ^ shift) for i in range(mp)]
        reward = reward + lax.ppermute(partial_reward, "mp", ring)
    return (reward, kept_blocks)


def solution(mesh):
    placed = (
        P("beam", None, "mp"),
        P("beam", None, None, "mp"),
        P("beam", None, None, "mp"),
        P("beam", None, None, "mp"),
        P(),
        P("beam", None),
        P("beam"),
        P(),
        P("mp"),
    )
    return jax.shard_map(
        on_device,
        mesh=mesh,
        in_specs=placed,
        out_specs=(P("beam", None), P("beam", None, None, "mp")),
        check_vma=False,
    )
```

```python
import functools
import math

import jax
import jax.numpy as jnp
from jax import lax
from jax.experimental import pallas as pl
from jax.experimental.pallas import tpu as pltpu
from jax.sharding import PartitionSpec as P

HEAD_SIZE = 128
CHILD = 2
LOG2_SCALE = HEAD_SIZE ** (-0.5) * math.log2(math.e)
MASKED = -1e30
SAFE_LOW = 2.0**-60
SAFE_HIGH = 2.0**100
LANES_BOTH = 2 * HEAD_SIZE
AHEAD = 4
IN_HBM = pl.BlockSpec(memory_space=pltpu.HBM)
IN_VMEM = pl.BlockSpec(memory_space=pltpu.VMEM)
ANY = pl.BlockSpec(memory_space=pl.ANY)


def dot_last(a, b):
    return lax.dot_general(
        a, b, (((1,), (1,)), ((), ())), preferred_element_type=jnp.float32
    )


def dot_first(a, b):
    return lax.dot_general(
        a, b, (((0,), (0,)), ((), ())), preferred_element_type=jnp.float32
    )


def one_hot_rows(rows, period, first):
    shape = (rows, LANES_BOTH)
    row = lax.broadcasted_iota(jnp.int32, shape, 0) % period
    head = first + lax.broadcasted_iota(jnp.int32, shape, 1) // HEAD_SIZE
    return jnp.where(row == head, 1.0, 0.0).astype(jnp.bfloat16)


def lane_rows(rows, period):
    shape = (rows, HEAD_SIZE)
    row = lax.broadcasted_iota(jnp.int32, shape, 0) % period
    lane = lax.broadcasted_iota(jnp.int32, shape, 1)
    return jnp.where(row == lane, 1.0, 0.0).astype(jnp.bfloat16)


def spread_columns(columns, first):
    shape = (columns.shape[0], HEAD_SIZE)
    return jnp.concatenate(
        [
            jnp.broadcast_to(columns[:, first : first + 1], shape),
            jnp.broadcast_to(columns[:, first + 1 : first + 2], shape),
        ],
        axis=1,
    )


def split_keys(keys):
    scaled = keys.astype(jnp.float32) * LOG2_SCALE
    high = scaled.astype(jnp.bfloat16)
    low = (scaled - high.astype(jnp.float32)).astype(jnp.bfloat16)
    return jnp.concatenate([high, low], axis=1)


def kv_lanes(kv):
    return slice(kv * HEAD_SIZE, (kv + 1) * HEAD_SIZE)


def query_pair(query, beam, pair):
    start = pair * LANES_BOTH
    return jnp.concatenate(
        [
            query[beam, :, start : start + HEAD_SIZE],
            query[beam, :, start + HEAD_SIZE : start + LANES_BOTH],
        ],
        axis=0,
    )


def weigh(scores, sums):
    weights = jnp.exp2(scores).reshape(-1, 8, LANES_BOTH)
    return (
        jnp.sum(weights * sums.reshape(weights.shape), axis=0),
        jnp.sum(weights, axis=0),
    )


def row_sum(x):
    return jnp.sum(x, axis=0, keepdims=True)


def causal(tokens):
    shape = (tokens, LANES_BOTH)
    key_pos = lax.broadcasted_iota(jnp.int32, shape, 0)
    token_pos = lax.broadcasted_iota(jnp.int32, shape, 1) % tokens
    return key_pos <= token_pos


def find_row(table, start, step, count, first, beam_dev):
    found = jnp.int32(0)
    for i in range(count):
        row = table[start + i * step] - first
        found = jnp.where((row >= 0) & (row < beam_dev), row, found)
    return found


def pack_kernel(own_ref, parent_ref, keep_ref, weight_ref, newest_ref, new_ref, *rest, beam_dev, keep_dev):
    devices = len(rest) - 3
    outs = rest[:devices]
    value_buf, value_sem, rest_sem = rest[devices:]
    groups = beam_dev // CHILD
    first = own_ref[0] * beam_dev
    tokens = newest_ref.shape[2]
    kv_heads = newest_ref.shape[3] // HEAD_SIZE
    per_group = weight_ref.shape[0] // kv_heads

    def loads(k, row, kept):
        out = outs[k]
        return (
            pltpu.make_async_copy(
                newest_ref.at[row, 1], value_buf.at[k], value_sem.at[k]
            ),
            pltpu.make_async_copy(
                newest_ref.at[row, 0],
                out.at[pl.ds(2 * tokens, tokens)],
                rest_sem.at[k, 0],
            ),
            pltpu.make_async_copy(
                new_ref.at[kept, 0], out.at[pl.ds(0, tokens)], rest_sem.at[k, 1]
            ),
            pltpu.make_async_copy(
                new_ref.at[kept, 1], out.at[pl.ds(tokens, tokens)], rest_sem.at[k, 2]
            ),
        )

    for k in range(devices):
        peer = own_ref[0] ^ k
        row = find_row(parent_ref, peer * beam_dev, CHILD, groups, first, beam_dev)
        kept = find_row(keep_ref, peer * keep_dev, 1, keep_dev, first, beam_dev)
        for copy in loads(k, row, kept):
            copy.start()
    for k in range(devices):
        value_copy = loads(k, 0, 0)[0]
        value_copy.wait()
        for kv in range(kv_heads):
            total = dot_last(
                weight_ref[kv * per_group : (kv + 1) * per_group],
                value_buf[k, :, kv_lanes(kv)],
            )
            high = total.astype(jnp.bfloat16)
            low = (total - high.astype(jnp.float32)).astype(jnp.bfloat16)
            outs[k][3 * tokens : 3 * tokens + per_group, kv_lanes(kv)] = high
            outs[k][3 * tokens + per_group :, kv_lanes(kv)] = low
    for k in range(devices):
        for copy in loads(k, 0, 0)[1:]:
            copy.wait()


def local_kernel(
    own_ref,
    block_ids,
    live_count,
    query_any,
    new_any,
    store_any,
    weight_ref,
    state_ref,
    query_buf,
    new_buf,
    store_buf,
    spread_ref,
    keys_ref,
    sums_ref,
    query_sem,
    new_sem,
    store_sem,
    *,
    pairs,
    pairs_kv,
    slots,
):
    beams, tokens = query_buf.shape[:2]
    blocks = store_buf.shape[1]
    heads = weight_ref.shape[0]
    kv_heads = pairs // pairs_kv
    depth = min(AHEAD, beams)

    def store_copies():
        return [
            pltpu.make_async_copy(
                store_any.at[:, side], store_buf.at[side], store_sem.at[side]
            )
            for side in (1, 0)
        ]

    def beam_copies(b):
        return (
            pltpu.make_async_copy(query_any.at[b], query_buf.at[b], query_sem.at[b]),
            pltpu.make_async_copy(new_any.at[b], new_buf.at[b], new_sem.at[b]),
        )

    for copy in store_copies():
        copy.start()
    for pair in range(pairs):
        spread_ref[pair] = dot_first(
            weight_ref[...], one_hot_rows(heads, heads, 2 * pair)
        ).astype(jnp.bfloat16)
    for copy in store_copies():
        copy.wait()
    for b in range(depth):
        for copy in beam_copies(b):
            copy.start()
    for pair in range(pairs):
        values = store_buf[1, :, :, kv_lanes(pair // pairs_kv)]
        sums_ref[pair] = jnp.dot(
            values.reshape(blocks * tokens, HEAD_SIZE),
            spread_ref[pair],
            preferred_element_type=jnp.float32,
        )

    @pl.loop(0, blocks)
    def _(block):
        for kv in range(kv_heads):
            keys_ref[block, kv] = split_keys(store_buf[0, block, :, kv_lanes(kv)])

    allowed = causal(tokens)
    turned = dot_first(weight_ref[...], lane_rows(heads, heads)).astype(jnp.bfloat16)

    def beam_body(b, count):
        ids = [block_ids[i, b] - own_ref[0] * blocks for i in range(count)]
        for kv in range(kv_heads):
            keys = [keys_ref[i, kv] for i in ids]
            keys = jnp.concatenate(
                keys + [split_keys(new_buf[b, 0, :, kv_lanes(kv)])], axis=0
            )
            columns = jnp.dot(
                new_buf[b, 1, :, kv_lanes(kv)], turned, preferred_element_type=jnp.float32
            )
            for pair in range(kv * pairs_kv, (kv + 1) * pairs_kv):
                own_sums = spread_columns(columns, 2 * pair)
                query = query_pair(query_buf, b, pair)
                scores = dot_last(keys, jnp.concatenate([query, query], axis=1))
                own_scores = jnp.where(allowed, scores[count * tokens :], MASKED)
                top, bottom = weigh(own_scores, own_sums)
                for i, block in enumerate(ids):
                    sums = sums_ref[pair, pl.ds(pl.multiple_of(block * tokens, tokens), tokens)]
                    more = weigh(scores[i * tokens : (i + 1) * tokens], sums)
                    top, bottom = top + more[0], bottom + more[1]
                state_ref[b, 0, pair : pair + 1] = row_sum(top)
                state_ref[b, 1, pair : pair + 1] = row_sum(bottom)

    @pl.loop(0, beams)
    def _(b):
        @pl.when(b + depth < beams)
        def _():
            for copy in beam_copies(b + depth):
                copy.start()

        for copy in beam_copies(b):
            copy.wait()
        for count in range(1, slots + 1):

            @pl.when(live_count[b] == count)
            def _():
                beam_body(b, count)


def parent_kernel(own_ref, parent_ref, keep_ref, block_ids, live_count, *rest, devices, pairs, pairs_kv):
    state_ref, weight_ref, query_buf, new_any, store_any = rest[:5]
    arrived = rest[5 : 5 + devices]
    reward_ref, kept_ref = rest[5 + devices : 7 + devices]
    (
        parent_buf,
        kept_buf,
        slow_block,
        slow_state,
        parent_sem,
        load_sem,
        store_sem,
        slow_sem,
    ) = rest[7 + devices :]
    beams, tokens = query_buf.shape[:2]
    own = own_ref[0]
    keep_dev = kept_ref.shape[0]
    kv_heads = pairs // pairs_kv
    blocks = store_any.shape[0]
    sum_rows = parent_buf.shape[1] - tokens
    heads = 2 * pairs

    def parent_load(k):
        return pltpu.make_async_copy(
            arrived[k].at[pl.ds(2 * tokens, tokens + sum_rows)],
            parent_buf.at[k],
            parent_sem.at[k],
        )

    def kept_load(k):
        return pltpu.make_async_copy(
            arrived[k].at[pl.ds(0, 2 * tokens)], kept_buf.at[k], load_sem.at[k]
        )

    def kept_stores(j, k):
        return [
            pltpu.make_async_copy(
                kept_buf.at[k, pl.ds(side * tokens, tokens)],
                kept_ref.at[j, side],
                store_sem.at[j, side],
            )
            for side in range(2)
        ]

    def slot_of(b):
        return (parent_ref[own * beams + b] // beams) ^ own

    for k in range(devices):
        parent_load(k).start()
    for k in range(devices):
        kept_load(k).start()
    for k in range(devices):
        parent_load(k).wait()

    def group_step(group, limits):
        slot = slot_of(group * CHILD)
        lowest, highest = limits
        totals = [jnp.zeros((1, tokens), jnp.float32) for _ in range(CHILD)]
        for kv in range(kv_heads):
            keys = parent_buf[slot, :tokens, kv_lanes(kv)]
            columns = dot_first(
                parent_buf[slot, tokens:, kv_lanes(kv)],
                lane_rows(sum_rows, sum_rows // 2),
            )
            for pair in range(kv * pairs_kv, (kv + 1) * pairs_kv):
                sums = spread_columns(columns, 2 * (pair % pairs_kv))
                for child in range(CHILD):
                    b = group * CHILD + child
                    query = query_pair(query_buf, b, pair)
                    scores = dot_last(keys, query) * LOG2_SCALE
                    top, bottom = weigh(scores, sums)
                    top = row_sum(top) + state_ref[b, 0, pair : pair + 1]
                    bottom = row_sum(bottom) + state_ref[b, 1, pair : pair + 1]
                    lowest = jnp.minimum(lowest, bottom)
                    highest = jnp.maximum(highest, bottom)
                    ratio = top / bottom
                    totals[child] += ratio[:, :tokens] + ratio[:, tokens:]
        for child in range(CHILD):
            reward_ref[pl.ds(group * CHILD + child, 1), :] = totals[child]
        return lowest, highest

    def start_kept():
        for k in range(devices):
            kept_load(k).wait()

        @pl.loop(0, keep_dev)
        def _(j):
            k = (keep_ref[own * keep_dev + j] // beams) ^ own
            for copy in kept_stores(j, k):
                copy.start()

    limits = (
        jnp.full((1, LANES_BOTH), SAFE_HIGH, jnp.float32),
        jnp.full((1, LANES_BOTH), SAFE_LOW, jnp.float32),
    )
    groups = beams // CHILD
    limits = lax.fori_loop(0, groups // 2, group_step, limits)
    start_kept()
    lowest, highest = lax.fori_loop(groups // 2, groups, group_step, limits)

    @pl.loop(0, keep_dev)
    def _(j):
        for copy in kept_stores(j, 0):
            copy.wait()

    def fetch(source, target):
        copy = pltpu.make_async_copy(source, target, slow_sem)
        copy.start()
        copy.wait()

    def online_step(b, pair, keys, sums, allowed=None):
        start = pl.multiple_of(pair * LANES_BOTH, LANES_BOTH)
        query = jnp.concatenate(
            [
                query_buf[b, :, pl.ds(start, HEAD_SIZE)],
                query_buf[b, :, pl.ds(start + HEAD_SIZE, HEAD_SIZE)],
            ],
            axis=0,
        )
        scores = dot_last(keys, query)
        if allowed is not None:
            scores = jnp.where(allowed, scores, MASKED)
        scores = scores.reshape(-1, 8, LANES_BOTH)
        before = slow_state[0, pair]
        after = jnp.maximum(before, jnp.max(scores, axis=0))
        fade = jnp.exp2((before - after) * LOG2_SCALE)
        weights = jnp.exp2((scores - after[None]) * LOG2_SCALE)
        sums = sums.reshape(weights.shape)
        slow_state[0, pair] = after
        slow_state[1, pair] = slow_state[1, pair] * fade + jnp.sum(weights * sums, axis=0)
        slow_state[2, pair] = slow_state[2, pair] * fade + jnp.sum(weights, axis=0)

    def slow_lanes(pair):
        return pl.ds(pl.multiple_of(pair // pairs_kv * HEAD_SIZE, HEAD_SIZE), HEAD_SIZE)

    def slow_plain(b, pair, allowed=None):
        spread = dot_first(weight_ref[...], one_hot_rows(heads, heads, 2 * pair))
        sums = jnp.dot(
            slow_block[1, :, slow_lanes(pair)],
            spread.astype(jnp.bfloat16),
            preferred_element_type=jnp.float32,
        )
        online_step(b, pair, slow_block[0, :, slow_lanes(pair)], sums, allowed)

    def slow_beam(b):
        slow_state[0] = jnp.full(slow_state.shape[1:], MASKED, jnp.float32)
        slow_state[1] = jnp.zeros(slow_state.shape[1:], jnp.float32)
        slow_state[2] = jnp.zeros(slow_state.shape[1:], jnp.float32)

        @pl.loop(0, live_count[b])
        def _(i):
            fetch(store_any.at[block_ids[i, b] - own * blocks], slow_block)
            pl.loop(0, pairs)(lambda pair: slow_plain(b, pair))

        fetch(new_any.at[b], slow_block)
        pl.loop(0, pairs)(lambda pair: slow_plain(b, pair, causal(tokens)))
        here = slot_of(b)
        reward_ref[pl.ds(b, 1), :] = jnp.zeros((1, tokens), jnp.float32)

        @pl.loop(0, pairs)
        def _(pair):
            sums = dot_first(
                parent_buf[here, tokens:, slow_lanes(pair)],
                one_hot_rows(sum_rows, sum_rows // 2, 2 * (pair % pairs_kv)),
            )
            online_step(b, pair, parent_buf[here, :tokens, slow_lanes(pair)], sums)
            state = slow_state[0, pair]
            row_max = jnp.max(state, axis=0, keepdims=True)
            fade = jnp.exp2((state - row_max) * LOG2_SCALE)
            ratio = jnp.sum(slow_state[1, pair] * fade, axis=0, keepdims=True) / jnp.sum(
                slow_state[2, pair] * fade, axis=0, keepdims=True
            )
            reward_ref[pl.ds(b, 1), :] += ratio[:, :tokens] + ratio[:, tokens:]

    low_ok = jnp.min(lowest) >= SAFE_LOW
    high_ok = jnp.max(highest) <= SAFE_HIGH

    @pl.when(jnp.logical_not(low_ok & high_ok))
    def _():
        pl.loop(0, beams)(slow_beam)


def on_device(
    queries,
    new_kv,
    newest_key_value,
    ancestor_block_store,
    parent,
    ancestors,
    ancestor_count,
    keep_list,
    w_reward,
):
    devices = lax.axis_size("beam")
    mp = lax.axis_size("mp")
    own = lax.axis_index("beam").reshape(1)
    beam_dev, _, tokens, kv_width = new_kv.shape
    q_width = queries.shape[2]
    heads = q_width // HEAD_SIZE
    kv_heads = kv_width // HEAD_SIZE
    per_group = heads // kv_heads
    pairs = heads // 2
    pairs_kv = pairs // kv_heads
    keep_dev = keep_list.shape[0] // devices
    blocks = ancestor_block_store.shape[0]
    pack_rows = 3 * tokens + 2 * per_group
    packed = jax.ShapeDtypeStruct((pack_rows, kv_width), new_kv.dtype)
    weight = w_reward.reshape(heads, HEAD_SIZE)
    weight_spec = pl.BlockSpec((heads, HEAD_SIZE), lambda i, *_: (0, 0))
    dma = pltpu.SemaphoreType.DMA

    sent = pl.pallas_call(
        functools.partial(pack_kernel, beam_dev=beam_dev, keep_dev=keep_dev),
        out_shape=(pltpu.VMEM(packed.shape, packed.dtype),) * devices,
        grid_spec=pltpu.PrefetchScalarGridSpec(
            num_scalar_prefetch=3,
            grid=(1,),
            in_specs=[weight_spec, IN_HBM, IN_HBM],
            out_specs=(IN_VMEM,) * devices,
            scratch_shapes=[
                pltpu.VMEM((devices, tokens, kv_width), jnp.bfloat16),
                dma((devices,)),
                dma((devices, 3)),
            ],
        ),
        name="pack",
    )(
        own,
        parent,
        keep_list,
        weight,
        pltpu.with_memory_space_constraint(newest_key_value, pltpu.HBM),
        pltpu.with_memory_space_constraint(new_kv, pltpu.HBM),
    )

    arrived = [sent[0]] + [None] * (devices - 1)
    for k in range(devices - 1, 0, -1):
        arrived[k] = lax.ppermute(sent[k], "beam", [(i, i ^ k) for i in range(devices)])

    state_shape = (beam_dev, 2, pairs, LANES_BOTH)
    state, near_queries = pl.pallas_call(
        functools.partial(
            local_kernel, pairs=pairs, pairs_kv=pairs_kv, slots=ancestors.shape[1]
        ),
        out_shape=(
            pltpu.VMEM(state_shape, jnp.float32),
            pltpu.VMEM(queries.shape, queries.dtype),
        ),
        grid_spec=pltpu.PrefetchScalarGridSpec(
            num_scalar_prefetch=3,
            grid=(1,),
            in_specs=[IN_HBM, IN_HBM, IN_HBM, weight_spec],
            out_specs=(IN_VMEM, IN_VMEM),
            scratch_shapes=[
                pltpu.VMEM(new_kv.shape, jnp.bfloat16),
                pltpu.VMEM((2, blocks, tokens, kv_width), jnp.bfloat16),
                pltpu.VMEM((pairs, HEAD_SIZE, LANES_BOTH), jnp.bfloat16),
                pltpu.VMEM((blocks, kv_heads, tokens, LANES_BOTH), jnp.bfloat16),
                pltpu.VMEM((pairs, blocks * tokens, LANES_BOTH), jnp.float32),
                dma((beam_dev,)),
                dma((beam_dev,)),
                dma((2,)),
            ],
        ),
        cost_estimate=pl.CostEstimate(
            flops=20_000_000_000, transcendentals=20_000_000, bytes_accessed=16_000_000
        ),
        compiler_params=pltpu.CompilerParams(vmem_limit_bytes=28 << 20),
        name="local",
    )(
        own,
        ancestors.T,
        ancestor_count,
        pltpu.with_memory_space_constraint(queries, pltpu.HBM),
        pltpu.with_memory_space_constraint(new_kv, pltpu.HBM),
        pltpu.with_memory_space_constraint(ancestor_block_store, pltpu.HBM),
        weight,
    )

    partial_reward, kept_blocks = pl.pallas_call(
        functools.partial(
            parent_kernel, devices=devices, pairs=pairs, pairs_kv=pairs_kv
        ),
        out_shape=(
            jax.ShapeDtypeStruct((beam_dev, tokens), jnp.float32),
            jax.ShapeDtypeStruct((keep_dev,) + new_kv.shape[1:], new_kv.dtype),
        ),
        grid_spec=pltpu.PrefetchScalarGridSpec(
            num_scalar_prefetch=5,
            grid=(1,),
            in_specs=[IN_VMEM, weight_spec, IN_VMEM, IN_HBM, IN_HBM] + [IN_VMEM] * devices,
            out_specs=(
                pl.BlockSpec((beam_dev, tokens), lambda i, *_: (0, 0)),
                ANY,
            ),
            scratch_shapes=[
                pltpu.VMEM((devices, tokens + 2 * per_group, kv_width), jnp.bfloat16),
                pltpu.VMEM((devices, 2 * tokens, kv_width), jnp.bfloat16),
                pltpu.VMEM((2, tokens, kv_width), jnp.bfloat16),
                pltpu.VMEM((3, pairs, 8, LANES_BOTH), jnp.float32),
                dma((devices,)),
                dma((devices,)),
                dma((keep_dev, 2)),
                dma(()),
            ],
        ),
        compiler_params=pltpu.CompilerParams(vmem_limit_bytes=16 << 20),
        name="parents",
    )(
        own,
        parent,
        keep_list,
        ancestors.T,
        ancestor_count,
        pltpu.with_memory_space_constraint(state, pltpu.VMEM),
        weight,
        pltpu.with_memory_space_constraint(near_queries, pltpu.VMEM),
        pltpu.with_memory_space_constraint(new_kv, pltpu.HBM),
        pltpu.with_memory_space_constraint(ancestor_block_store, pltpu.HBM),
        *[pltpu.with_memory_space_constraint(x, pltpu.VMEM) for x in arrived],
    )

    reward = partial_reward
    for shift in range(1, mp):
        ring = [(i, i ^ shift) for i in range(mp)]
        reward = reward + lax.ppermute(partial_reward, "mp", ring)
    return (reward, kept_blocks)


def solution(mesh):
    placed = (
        P("beam", None, "mp"),
        P("beam", None, None, "mp"),
        P("beam", None, None, "mp"),
        P("beam", None, None, "mp"),
        P(),
        P("beam", None),
        P("beam"),
        P(),
        P("mp"),
    )
    return jax.shard_map(
        on_device,
        mesh=mesh,
        in_specs=placed,
        out_specs=(P("beam", None), P("beam", None, None, "mp")),
        check_vma=False,
    )
```

```python
import functools
import math

import jax
import jax.numpy as jnp
from jax import lax
from jax.experimental import pallas as pl
from jax.experimental.pallas import tpu as pltpu
from jax.sharding import PartitionSpec as P

HEAD_SIZE = 128
CHILD = 2
LOG2_SCALE = HEAD_SIZE ** (-0.5) * math.log2(math.e)
MASKED = -1e30
SAFE_LOW = 2.0**-60
SAFE_HIGH = 2.0**100
LANES_BOTH = 2 * HEAD_SIZE
AHEAD = 4
IN_HBM = pl.BlockSpec(memory_space=pltpu.HBM)
IN_VMEM = pl.BlockSpec(memory_space=pltpu.VMEM)
ANY = pl.BlockSpec(memory_space=pl.ANY)


def dot_last(a, b):
    return lax.dot_general(
        a, b, (((1,), (1,)), ((), ())), preferred_element_type=jnp.float32
    )


def dot_first(a, b):
    return lax.dot_general(
        a, b, (((0,), (0,)), ((), ())), preferred_element_type=jnp.float32
    )


def one_hot_rows(rows, period, first):
    shape = (rows, LANES_BOTH)
    row = lax.broadcasted_iota(jnp.int32, shape, 0) % period
    head = first + lax.broadcasted_iota(jnp.int32, shape, 1) // HEAD_SIZE
    return jnp.where(row == head, 1.0, 0.0).astype(jnp.bfloat16)


def lane_rows(rows, period):
    shape = (rows, HEAD_SIZE)
    row = lax.broadcasted_iota(jnp.int32, shape, 0) % period
    lane = lax.broadcasted_iota(jnp.int32, shape, 1)
    return jnp.where(row == lane, 1.0, 0.0).astype(jnp.bfloat16)


def spread_columns(columns, first):
    shape = (columns.shape[0], HEAD_SIZE)
    return jnp.concatenate(
        [
            jnp.broadcast_to(columns[:, first : first + 1], shape),
            jnp.broadcast_to(columns[:, first + 1 : first + 2], shape),
        ],
        axis=1,
    )


def split_keys(keys):
    scaled = keys.astype(jnp.float32) * LOG2_SCALE
    high = scaled.astype(jnp.bfloat16)
    low = (scaled - high.astype(jnp.float32)).astype(jnp.bfloat16)
    return jnp.concatenate([high, low], axis=1)


def kv_lanes(kv):
    return slice(kv * HEAD_SIZE, (kv + 1) * HEAD_SIZE)


def query_pair(query, beam, pair):
    start = pair * LANES_BOTH
    return jnp.concatenate(
        [
            query[beam, :, start : start + HEAD_SIZE],
            query[beam, :, start + HEAD_SIZE : start + LANES_BOTH],
        ],
        axis=0,
    )


def weigh(scores, sums):
    weights = jnp.exp2(scores).reshape(-1, 8, LANES_BOTH)
    return (
        jnp.sum(weights * sums.reshape(weights.shape), axis=0),
        jnp.sum(weights, axis=0),
    )


def row_sum(x):
    return jnp.sum(x, axis=0, keepdims=True)


def causal(tokens):
    shape = (tokens, LANES_BOTH)
    key_pos = lax.broadcasted_iota(jnp.int32, shape, 0)
    token_pos = lax.broadcasted_iota(jnp.int32, shape, 1) % tokens
    return key_pos <= token_pos


def find_row(table, start, step, count, first, beam_dev):
    found = jnp.int32(0)
    for i in range(count):
        row = table[start + i * step] - first
        found = jnp.where((row >= 0) & (row < beam_dev), row, found)
    return found


def pack_kernel(own_ref, parent_ref, keep_ref, weight_ref, newest_ref, new_ref, *rest, beam_dev, keep_dev):
    devices = len(rest) - 3
    outs = rest[:devices]
    value_buf, value_sem, rest_sem = rest[devices:]
    groups = beam_dev // CHILD
    first = own_ref[0] * beam_dev
    tokens = newest_ref.shape[2]
    kv_heads = newest_ref.shape[3] // HEAD_SIZE
    per_group = weight_ref.shape[0] // kv_heads

    def loads(k, row, kept):
        out = outs[k]
        return (
            pltpu.make_async_copy(
                newest_ref.at[row, 1], value_buf.at[k], value_sem.at[k]
            ),
            pltpu.make_async_copy(
                newest_ref.at[row, 0],
                out.at[pl.ds(2 * tokens, tokens)],
                rest_sem.at[k, 0],
            ),
            pltpu.make_async_copy(
                new_ref.at[kept, 0], out.at[pl.ds(0, tokens)], rest_sem.at[k, 1]
            ),
            pltpu.make_async_copy(
                new_ref.at[kept, 1], out.at[pl.ds(tokens, tokens)], rest_sem.at[k, 2]
            ),
        )

    for k in range(devices):
        peer = own_ref[0] ^ k
        row = find_row(parent_ref, peer * beam_dev, CHILD, groups, first, beam_dev)
        kept = find_row(keep_ref, peer * keep_dev, 1, keep_dev, first, beam_dev)
        for copy in loads(k, row, kept):
            copy.start()
    for k in range(devices):
        value_copy = loads(k, 0, 0)[0]
        value_copy.wait()
        for kv in range(kv_heads):
            total = dot_last(
                weight_ref[kv * per_group : (kv + 1) * per_group],
                value_buf[k, :, kv_lanes(kv)],
            )
            high = total.astype(jnp.bfloat16)
            low = (total - high.astype(jnp.float32)).astype(jnp.bfloat16)
            outs[k][3 * tokens : 3 * tokens + per_group, kv_lanes(kv)] = high
            outs[k][3 * tokens + per_group :, kv_lanes(kv)] = low
    for k in range(devices):
        for copy in loads(k, 0, 0)[1:]:
            copy.wait()


def local_kernel(
    own_ref,
    block_ids,
    live_count,
    query_any,
    new_any,
    store_any,
    weight_ref,
    state_ref,
    query_buf,
    new_buf,
    store_buf,
    spread_ref,
    keys_ref,
    sums_ref,
    query_sem,
    new_sem,
    store_sem,
    *,
    pairs,
    pairs_kv,
    slots,
):
    beams, tokens = query_buf.shape[:2]
    blocks = store_buf.shape[1]
    heads = weight_ref.shape[0]
    kv_heads = pairs // pairs_kv
    depth = min(AHEAD, beams)

    def store_copies():
        return [
            pltpu.make_async_copy(
                store_any.at[:, side], store_buf.at[side], store_sem.at[side]
            )
            for side in (1, 0)
        ]

    def beam_copies(b):
        return (
            pltpu.make_async_copy(query_any.at[b], query_buf.at[b], query_sem.at[b]),
            pltpu.make_async_copy(new_any.at[b], new_buf.at[b], new_sem.at[b]),
        )

    for copy in store_copies():
        copy.start()
    for pair in range(pairs):
        spread_ref[pair] = dot_first(
            weight_ref[...], one_hot_rows(heads, heads, 2 * pair)
        ).astype(jnp.bfloat16)
    values_copy, keys_copy = store_copies()
    values_copy.wait()
    for b in range(depth):
        for copy in beam_copies(b):
            copy.start()
    for pair in range(pairs):
        values = store_buf[1, :, :, kv_lanes(pair // pairs_kv)]
        sums_ref[pair] = jnp.dot(
            values.reshape(blocks * tokens, HEAD_SIZE),
            spread_ref[pair],
            preferred_element_type=jnp.float32,
        )

    keys_copy.wait()

    @pl.loop(0, blocks)
    def _(block):
        for kv in range(kv_heads):
            keys_ref[block, kv] = split_keys(store_buf[0, block, :, kv_lanes(kv)])

    allowed = causal(tokens)
    turned = dot_first(weight_ref[...], lane_rows(heads, heads)).astype(jnp.bfloat16)

    def beam_body(b, count):
        ids = [block_ids[i, b] - own_ref[0] * blocks for i in range(count)]
        for kv in range(kv_heads):
            keys = [keys_ref[i, kv] for i in ids]
            keys = jnp.concatenate(
                keys + [split_keys(new_buf[b, 0, :, kv_lanes(kv)])], axis=0
            )
            columns = jnp.dot(
                new_buf[b, 1, :, kv_lanes(kv)], turned, preferred_element_type=jnp.float32
            )
            for pair in range(kv * pairs_kv, (kv + 1) * pairs_kv):
                own_sums = spread_columns(columns, 2 * pair)
                query = query_pair(query_buf, b, pair)
                scores = dot_last(keys, jnp.concatenate([query, query], axis=1))
                own_scores = jnp.where(allowed, scores[count * tokens :], MASKED)
                top, bottom = weigh(own_scores, own_sums)
                for i, block in enumerate(ids):
                    sums = sums_ref[pair, pl.ds(pl.multiple_of(block * tokens, tokens), tokens)]
                    more = weigh(scores[i * tokens : (i + 1) * tokens], sums)
                    top, bottom = top + more[0], bottom + more[1]
                state_ref[b, 0, pair : pair + 1] = row_sum(top)
                state_ref[b, 1, pair : pair + 1] = row_sum(bottom)

    @pl.loop(0, beams)
    def _(b):
        @pl.when(b + depth < beams)
        def _():
            for copy in beam_copies(b + depth):
                copy.start()

        for copy in beam_copies(b):
            copy.wait()
        for count in range(1, slots + 1):

            @pl.when(live_count[b] == count)
            def _():
                beam_body(b, count)


def parent_kernel(own_ref, parent_ref, keep_ref, block_ids, live_count, *rest, devices, pairs, pairs_kv):
    state_ref, weight_ref, query_buf, new_any, store_any = rest[:5]
    arrived = rest[5 : 5 + devices]
    reward_ref, kept_ref = rest[5 + devices : 7 + devices]
    (
        parent_buf,
        kept_buf,
        slow_block,
        slow_state,
        parent_sem,
        load_sem,
        store_sem,
        slow_sem,
    ) = rest[7 + devices :]
    beams, tokens = query_buf.shape[:2]
    own = own_ref[0]
    keep_dev = kept_ref.shape[0]
    kv_heads = pairs // pairs_kv
    blocks = store_any.shape[0]
    sum_rows = parent_buf.shape[1] - tokens
    heads = 2 * pairs

    def parent_load(k):
        return pltpu.make_async_copy(
            arrived[k].at[pl.ds(2 * tokens, tokens + sum_rows)],
            parent_buf.at[k],
            parent_sem.at[k],
        )

    def kept_load(k):
        return pltpu.make_async_copy(
            arrived[k].at[pl.ds(0, 2 * tokens)], kept_buf.at[k], load_sem.at[k]
        )

    def kept_stores(j, k):
        return [
            pltpu.make_async_copy(
                kept_buf.at[k, pl.ds(side * tokens, tokens)],
                kept_ref.at[j, side],
                store_sem.at[j, side],
            )
            for side in range(2)
        ]

    def slot_of(b):
        return (parent_ref[own * beams + b] // beams) ^ own

    for k in range(devices):
        parent_load(k).start()
    for k in range(devices):
        kept_load(k).start()
    for k in range(devices):
        parent_load(k).wait()

    def group_step(group, limits):
        slot = slot_of(group * CHILD)
        lowest, highest = limits
        totals = [jnp.zeros((1, tokens), jnp.float32) for _ in range(CHILD)]
        for kv in range(kv_heads):
            keys = parent_buf[slot, :tokens, kv_lanes(kv)]
            columns = dot_first(
                parent_buf[slot, tokens:, kv_lanes(kv)],
                lane_rows(sum_rows, sum_rows // 2),
            )
            for pair in range(kv * pairs_kv, (kv + 1) * pairs_kv):
                sums = spread_columns(columns, 2 * (pair % pairs_kv))
                for child in range(CHILD):
                    b = group * CHILD + child
                    query = query_pair(query_buf, b, pair)
                    scores = dot_last(keys, query) * LOG2_SCALE
                    top, bottom = weigh(scores, sums)
                    top = row_sum(top) + state_ref[b, 0, pair : pair + 1]
                    bottom = row_sum(bottom) + state_ref[b, 1, pair : pair + 1]
                    lowest = jnp.minimum(lowest, bottom)
                    highest = jnp.maximum(highest, bottom)
                    ratio = top / bottom
                    totals[child] += ratio[:, :tokens] + ratio[:, tokens:]
        for child in range(CHILD):
            reward_ref[pl.ds(group * CHILD + child, 1), :] = totals[child]
        return lowest, highest

    def start_kept():
        for k in range(devices):
            kept_load(k).wait()

        @pl.loop(0, keep_dev)
        def _(j):
            k = (keep_ref[own * keep_dev + j] // beams) ^ own
            for copy in kept_stores(j, k):
                copy.start()

    limits = (
        jnp.full((1, LANES_BOTH), SAFE_HIGH, jnp.float32),
        jnp.full((1, LANES_BOTH), SAFE_LOW, jnp.float32),
    )
    groups = beams // CHILD
    limits = lax.fori_loop(0, groups // 2, group_step, limits)
    start_kept()
    lowest, highest = lax.fori_loop(groups // 2, groups, group_step, limits)

    @pl.loop(0, keep_dev)
    def _(j):
        for copy in kept_stores(j, 0):
            copy.wait()

    def fetch(source, target):
        copy = pltpu.make_async_copy(source, target, slow_sem)
        copy.start()
        copy.wait()

    def online_step(b, pair, keys, sums, allowed=None):
        start = pl.multiple_of(pair * LANES_BOTH, LANES_BOTH)
        query = jnp.concatenate(
            [
                query_buf[b, :, pl.ds(start, HEAD_SIZE)],
                query_buf[b, :, pl.ds(start + HEAD_SIZE, HEAD_SIZE)],
            ],
            axis=0,
        )
        scores = dot_last(keys, query)
        if allowed is not None:
            scores = jnp.where(allowed, scores, MASKED)
        scores = scores.reshape(-1, 8, LANES_BOTH)
        before = slow_state[0, pair]
        after = jnp.maximum(before, jnp.max(scores, axis=0))
        fade = jnp.exp2((before - after) * LOG2_SCALE)
        weights = jnp.exp2((scores - after[None]) * LOG2_SCALE)
        sums = sums.reshape(weights.shape)
        slow_state[0, pair] = after
        slow_state[1, pair] = slow_state[1, pair] * fade + jnp.sum(weights * sums, axis=0)
        slow_state[2, pair] = slow_state[2, pair] * fade + jnp.sum(weights, axis=0)

    def slow_lanes(pair):
        return pl.ds(pl.multiple_of(pair // pairs_kv * HEAD_SIZE, HEAD_SIZE), HEAD_SIZE)

    def slow_plain(b, pair, allowed=None):
        spread = dot_first(weight_ref[...], one_hot_rows(heads, heads, 2 * pair))
        sums = jnp.dot(
            slow_block[1, :, slow_lanes(pair)],
            spread.astype(jnp.bfloat16),
            preferred_element_type=jnp.float32,
        )
        online_step(b, pair, slow_block[0, :, slow_lanes(pair)], sums, allowed)

    def slow_beam(b):
        slow_state[0] = jnp.full(slow_state.shape[1:], MASKED, jnp.float32)
        slow_state[1] = jnp.zeros(slow_state.shape[1:], jnp.float32)
        slow_state[2] = jnp.zeros(slow_state.shape[1:], jnp.float32)

        @pl.loop(0, live_count[b])
        def _(i):
            fetch(store_any.at[block_ids[i, b] - own * blocks], slow_block)
            pl.loop(0, pairs)(lambda pair: slow_plain(b, pair))

        fetch(new_any.at[b], slow_block)
        pl.loop(0, pairs)(lambda pair: slow_plain(b, pair, causal(tokens)))
        here = slot_of(b)
        reward_ref[pl.ds(b, 1), :] = jnp.zeros((1, tokens), jnp.float32)

        @pl.loop(0, pairs)
        def _(pair):
            sums = dot_first(
                parent_buf[here, tokens:, slow_lanes(pair)],
                one_hot_rows(sum_rows, sum_rows // 2, 2 * (pair % pairs_kv)),
            )
            online_step(b, pair, parent_buf[here, :tokens, slow_lanes(pair)], sums)
            state = slow_state[0, pair]
            row_max = jnp.max(state, axis=0, keepdims=True)
            fade = jnp.exp2((state - row_max) * LOG2_SCALE)
            ratio = jnp.sum(slow_state[1, pair] * fade, axis=0, keepdims=True) / jnp.sum(
                slow_state[2, pair] * fade, axis=0, keepdims=True
            )
            reward_ref[pl.ds(b, 1), :] += ratio[:, :tokens] + ratio[:, tokens:]

    low_ok = jnp.min(lowest) >= SAFE_LOW
    high_ok = jnp.max(highest) <= SAFE_HIGH

    @pl.when(jnp.logical_not(low_ok & high_ok))
    def _():
        pl.loop(0, beams)(slow_beam)


def on_device(
    queries,
    new_kv,
    newest_key_value,
    ancestor_block_store,
    parent,
    ancestors,
    ancestor_count,
    keep_list,
    w_reward,
):
    devices = lax.axis_size("beam")
    mp = lax.axis_size("mp")
    own = lax.axis_index("beam").reshape(1)
    beam_dev, _, tokens, kv_width = new_kv.shape
    q_width = queries.shape[2]
    heads = q_width // HEAD_SIZE
    kv_heads = kv_width // HEAD_SIZE
    per_group = heads // kv_heads
    pairs = heads // 2
    pairs_kv = pairs // kv_heads
    keep_dev = keep_list.shape[0] // devices
    blocks = ancestor_block_store.shape[0]
    pack_rows = 3 * tokens + 2 * per_group
    packed = jax.ShapeDtypeStruct((pack_rows, kv_width), new_kv.dtype)
    weight = w_reward.reshape(heads, HEAD_SIZE)
    weight_spec = pl.BlockSpec((heads, HEAD_SIZE), lambda i, *_: (0, 0))
    dma = pltpu.SemaphoreType.DMA

    sent = pl.pallas_call(
        functools.partial(pack_kernel, beam_dev=beam_dev, keep_dev=keep_dev),
        out_shape=(pltpu.VMEM(packed.shape, packed.dtype),) * devices,
        grid_spec=pltpu.PrefetchScalarGridSpec(
            num_scalar_prefetch=3,
            grid=(1,),
            in_specs=[weight_spec, IN_HBM, IN_HBM],
            out_specs=(IN_VMEM,) * devices,
            scratch_shapes=[
                pltpu.VMEM((devices, tokens, kv_width), jnp.bfloat16),
                dma((devices,)),
                dma((devices, 3)),
            ],
        ),
        name="pack",
    )(
        own,
        parent,
        keep_list,
        weight,
        pltpu.with_memory_space_constraint(newest_key_value, pltpu.HBM),
        pltpu.with_memory_space_constraint(new_kv, pltpu.HBM),
    )

    arrived = [sent[0]] + [None] * (devices - 1)
    for k in range(devices - 1, 0, -1):
        arrived[k] = lax.ppermute(sent[k], "beam", [(i, i ^ k) for i in range(devices)])

    state_shape = (beam_dev, 2, pairs, LANES_BOTH)
    state, near_queries = pl.pallas_call(
        functools.partial(
            local_kernel, pairs=pairs, pairs_kv=pairs_kv, slots=ancestors.shape[1]
        ),
        out_shape=(
            pltpu.VMEM(state_shape, jnp.float32),
            pltpu.VMEM(queries.shape, queries.dtype),
        ),
        grid_spec=pltpu.PrefetchScalarGridSpec(
            num_scalar_prefetch=3,
            grid=(1,),
            in_specs=[IN_HBM, IN_HBM, IN_HBM, weight_spec],
            out_specs=(IN_VMEM, IN_VMEM),
            scratch_shapes=[
                pltpu.VMEM(new_kv.shape, jnp.bfloat16),
                pltpu.VMEM((2, blocks, tokens, kv_width), jnp.bfloat16),
                pltpu.VMEM((pairs, HEAD_SIZE, LANES_BOTH), jnp.bfloat16),
                pltpu.VMEM((blocks, kv_heads, tokens, LANES_BOTH), jnp.bfloat16),
                pltpu.VMEM((pairs, blocks * tokens, LANES_BOTH), jnp.float32),
                dma((beam_dev,)),
                dma((beam_dev,)),
                dma((2,)),
            ],
        ),
        cost_estimate=pl.CostEstimate(
            flops=20_000_000_000, transcendentals=20_000_000, bytes_accessed=16_000_000
        ),
        compiler_params=pltpu.CompilerParams(vmem_limit_bytes=28 << 20),
        name="local",
    )(
        own,
        ancestors.T,
        ancestor_count,
        pltpu.with_memory_space_constraint(queries, pltpu.HBM),
        pltpu.with_memory_space_constraint(new_kv, pltpu.HBM),
        pltpu.with_memory_space_constraint(ancestor_block_store, pltpu.HBM),
        weight,
    )

    partial_reward, kept_blocks = pl.pallas_call(
        functools.partial(
            parent_kernel, devices=devices, pairs=pairs, pairs_kv=pairs_kv
        ),
        out_shape=(
            jax.ShapeDtypeStruct((beam_dev, tokens), jnp.float32),
            jax.ShapeDtypeStruct((keep_dev,) + new_kv.shape[1:], new_kv.dtype),
        ),
        grid_spec=pltpu.PrefetchScalarGridSpec(
            num_scalar_prefetch=5,
            grid=(1,),
            in_specs=[IN_VMEM, weight_spec, IN_VMEM, IN_HBM, IN_HBM] + [IN_VMEM] * devices,
            out_specs=(
                pl.BlockSpec((beam_dev, tokens), lambda i, *_: (0, 0)),
                ANY,
            ),
            scratch_shapes=[
                pltpu.VMEM((devices, tokens + 2 * per_group, kv_width), jnp.bfloat16),
                pltpu.VMEM((devices, 2 * tokens, kv_width), jnp.bfloat16),
                pltpu.VMEM((2, tokens, kv_width), jnp.bfloat16),
                pltpu.VMEM((3, pairs, 8, LANES_BOTH), jnp.float32),
                dma((devices,)),
                dma((devices,)),
                dma((keep_dev, 2)),
                dma(()),
            ],
        ),
        compiler_params=pltpu.CompilerParams(vmem_limit_bytes=16 << 20),
        name="parents",
    )(
        own,
        parent,
        keep_list,
        ancestors.T,
        ancestor_count,
        pltpu.with_memory_space_constraint(state, pltpu.VMEM),
        weight,
        pltpu.with_memory_space_constraint(near_queries, pltpu.VMEM),
        pltpu.with_memory_space_constraint(new_kv, pltpu.HBM),
        pltpu.with_memory_space_constraint(ancestor_block_store, pltpu.HBM),
        *[pltpu.with_memory_space_constraint(x, pltpu.VMEM) for x in arrived],
    )

    reward = partial_reward
    for shift in range(mp - 1, 0, -1):
        ring = [(i, i ^ shift) for i in range(mp)]
        reward = reward + lax.ppermute(partial_reward, "mp", ring)
    return (reward, kept_blocks)


def solution(mesh):
    placed = (
        P("beam", None, "mp"),
        P("beam", None, None, "mp"),
        P("beam", None, None, "mp"),
        P("beam", None, None, "mp"),
        P(),
        P("beam", None),
        P("beam"),
        P(),
        P("mp"),
    )
    return jax.shard_map(
        on_device,
        mesh=mesh,
        in_specs=placed,
        out_specs=(P("beam", None), P("beam", None, None, "mp")),
        check_vma=False,
    )
```
